512 devices in a mesh: wide: 64 (over x, z), narrow: 8 (over y, core).
Axes of the slice: x: 4, y: 4, z: 16, core: 2. Of those that a mesh axis runs over, the one named last changes fastest.
Arguments:
- tokens: bfloat16 [4096, 2, 5120], P('wide', None, 'narrow'), may hold values from -6 to 6
- qkv_weight: bfloat16 [5120, 6144], P('wide', 'narrow'), may hold values from -0.078125 to 0.078125
- rotated_prefix_keys: bfloat16 [64, 2048, 1024], P('wide', None, 'narrow'), may hold values from -120 to 120
- shared_prefix_values: bfloat16 [64, 2048, 1024], P('wide', None, 'narrow'), may hold values from -6 to 6
- prefix_of: int32 [4096, 1], P('wide'), may hold values from 0 to 63; in each aligned block of 64 rows (0 to 63, 64 to 127, ...) at most 2 rows name the same one
- positions: int32 [4096], P('wide'), may hold values from 512 to 2048, as said below
Outputs:
- attended: bfloat16 [4096, 2, 4096], P('wide', None, 'narrow')
The draws below stay inside these ranges and needn't reach their ends.
Inputs may be any that keep to these rules, and one draw needn't show every extreme that they name: `prefix_of`: the 64 requests of one index of wide name each prefix at most 2 times, a bound that some block reaches. The new tokens of request r sit at positions[r] + s.
All inputs are finite; a program needn't handle non-finite values.
Results may differ from the reference program's by a relative error of at most 0.012.
The reference program's roundings to bfloat16 on the way count: a program that leaves them out, or rounds other values in their place, can miss the bound.
Values may be sent and summed in bfloat16 or wider, within the bound.
A program may use at most 64 MiB of HBM per device.

```python
import math
import jax
import jax.numpy as jnp
import numpy as np
from jax import lax

D = 5120
QUERY_HEADS = 32
KEY_VALUE_HEADS = 8
HEAD_SIZE = 128
PREFIX_LENGTH = 2048
R_DEV = 64
DECODE_STEPS = 2
CAP = 2
COLS = 6144
SHARED_PREFIXES = 64
REQUEST_COUNT = 4096


def draw_positions(key, part):
    counts = jax.random.randint(key, (REQUEST_COUNT,), PREFIX_LENGTH // 4, PREFIX_LENGTH + 1)
    return counts.at[0].set(PREFIX_LENGTH).astype(jnp.int32)


def draw_rotated_prefix_keys(key, part):
    first_index = jax.random.fold_in(key, 0)
    value_block = jax.random.normal(first_index, (SHARED_PREFIXES, PREFIX_LENGTH, KEY_VALUE_HEADS * HEAD_SIZE), jnp.float32)
    return jnp.clip(value_block, -120.0, 120.0).astype(jnp.bfloat16)


def block_scale(rng, dims, cuts, low, top_value):
    def one(position, parts):
        steps = jax.random.uniform(jax.random.fold_in(jax.random.fold_in(rng, 6), position), (parts,), jnp.float32, low / len(cuts), top_value / len(cuts))
        return jnp.repeat(jnp.exp(steps), dims[position] // parts).reshape((-1,) + (1,) * (len(dims) - position - 1))

    gain = one(*cuts[0])
    for cut in cuts[1:]:
        gain = gain * one(*cut)
    return gain


def shared_out(stream_key, own, number, rows, count, top, reach, lean):
    order = jax.random.permutation(stream_key, count)
    heavy_load, common = shares(count, rows * top, reach, lean, True), shares(count, rows * top, reach, lean, False)
    places = jnp.arange(count)

    def named(lengths, offset_by):
        used = int((lengths > 0).sum())
        fixed = max(1, used // 4)
        passed = fixed + (places - fixed + offset_by * (used - fixed)) % max(1, count - fixed)
        return jnp.zeros((count,), jnp.int32).at[order[jnp.where(places < fixed, places, passed)]].set(jnp.asarray(lengths, jnp.int32))

    lengths = jnp.where(number % 4 == 0, named(heavy_load, number // 4), named(common, number - number // 4 - 1))
    mixed = jax.random.permutation(jax.random.fold_in(own, 3), count)
    source_of, taker = mixed[0:count // 2 * 2:2], mixed[1:count // 2 * 2:2]
    slack = jnp.minimum(lengths[source_of] - 1, reach - lengths[taker]) // 2
    slack = jnp.where((source_of == order[0]) | (taker == order[0]) | (lengths[taker] == 0), 0, jnp.maximum(slack, 0))
    passed = jax.random.randint(jax.random.fold_in(own, 4), (count // 2,), 0, 1 << 20) % (slack + 1)
    lengths = lengths.at[source_of].add(-passed).at[taker].add(passed)
    items = jnp.searchsorted(jnp.cumsum(lengths), jnp.arange(rows * top), side="right").astype(jnp.int32)
    table = items.reshape(top, rows).T
    table = table[jax.random.permutation(jax.random.fold_in(own, 1), rows)]
    offset_by = jax.random.randint(jax.random.fold_in(own, 2), (rows, 1), 0, top)
    return jnp.take_along_axis(table, (jnp.arange(top)[None, :] + offset_by) % top, axis=1)


def shares(count, total, most, lean, full):
    portions = [(1 << 20) // math.isqrt(rank ** lean) + 1 for rank in range(1, count + 1)]
    largest = most if full else min(most, max(-(-total // count), total * portions[0] // sum(portions)))
    least = 1 if total - largest >= count - 1 else 0
    holding, spare = [largest] + [least] * (count - 1), total - largest - least * (count - 1)
    while spare > 0:
        movable = [i for i in range(1, count) if holding[i] < largest] or [i for i in range(1, count) if holding[i] < most]
        mass, remaining = sum([portions[i] for i in movable]), spare
        for i in movable:
            addition = min(most - holding[i], max(1, remaining * portions[i] // mass), spare)
            holding[i] = holding[i] + addition
            spare = spare - addition
    return np.array(holding)


def scatter_about(key, shape, scale, bound, cuts=(), held_as=jnp.bfloat16):
    values = jax.random.normal(key, shape, jnp.float32) * scale
    if len(cuts) > 0:
        values = block_scale(key, shape, cuts, -0.22, 0.18) * values
    return jnp.clip(values, min=-bound, max=bound).astype(held_as)


def setup_inputs(seed: int = 0) -> dict:
    key_list = jax.random.split(jax.random.key(seed), 7)
    tokens = scatter_about(key_list[0], (REQUEST_COUNT, DECODE_STEPS, D), 1.0, 6.0, ((0, 64), (2, 8)))
    qkv_weight = scatter_about(key_list[1], (D, COLS), D ** -0.5, 0.078125, ((0, 64), (1, 8)))
    rotated_prefix_keys = draw_rotated_prefix_keys(jax.random.fold_in(key_list[6], 71), 0)
    shared_prefix_values = scatter_about(key_list[3], (SHARED_PREFIXES, PREFIX_LENGTH, KEY_VALUE_HEADS * HEAD_SIZE), 1.0, 6.0, ((0, 64), (2, 8)))
    prefix_of_keys = jax.random.split(jax.random.fold_in(key_list[4], 1), REQUEST_COUNT // R_DEV)
    prefix_of_turns = jax.random.permutation(jax.random.fold_in(key_list[4], 3), REQUEST_COUNT // R_DEV)
    prefix_of = jax.vmap(lambda own, number: shared_out(jax.random.fold_in(key_list[4], 2), own, number, R_DEV, SHARED_PREFIXES, 1, CAP, 2))(prefix_of_keys, prefix_of_turns).reshape((REQUEST_COUNT, 1))
    positions = draw_positions(jax.random.fold_in(key_list[6], 71), 0)
    return {"tokens": tokens, "qkv_weight": qkv_weight, "rotated_prefix_keys": rotated_prefix_keys, "shared_prefix_values": shared_prefix_values, "prefix_of": prefix_of, "positions": positions}


def rotate(value_block, where):
    half = HEAD_SIZE // 2
    freq = 10000.0 ** (-(jnp.arange(half, dtype=jnp.float32) * 2.0 / HEAD_SIZE))
    angle = where[..., None].astype(jnp.float32) * freq
    cosine = jnp.cos(angle)
    sine = jnp.sin(angle)
    first_index = value_block[..., :half]
    second = value_block[..., half:]
    return jnp.concatenate([first_index * cosine - second * sine, second * cosine + first_index * sine], axis=-1)


def reference(tokens, qkv_weight, rotated_prefix_keys, shared_prefix_values, prefix_of, positions):
    query_group = QUERY_HEADS // KEY_VALUE_HEADS
    flat = tokens.reshape(REQUEST_COUNT * DECODE_STEPS, D)
    mixed_output = jnp.dot(flat, qkv_weight, preferred_element_type=jnp.float32)
    mixed_output = mixed_output.reshape(REQUEST_COUNT, DECODE_STEPS, KEY_VALUE_HEADS, query_group + 2, HEAD_SIZE)
    where = positions[:, None] + jnp.arange(DECODE_STEPS, dtype=jnp.int32)[None, :]
    query = rotate(mixed_output[:, :, :, :query_group, :], where[:, :, None, None]).astype(jnp.bfloat16)
    own_key = rotate(mixed_output[:, :, :, query_group, :], where[:, :, None]).astype(jnp.bfloat16)
    own_value = mixed_output[:, :, :, query_group + 1, :].astype(jnp.bfloat16)
    block_slice = 16
    scale = 1.0 / (HEAD_SIZE ** 0.5)

    def attend(index):
        start = (index * block_slice).astype(jnp.int32)
        q_block = lax.dynamic_slice_in_dim(query, start, block_slice, 0).astype(jnp.float32)
        k_block = lax.dynamic_slice_in_dim(own_key, start, block_slice, 0).astype(jnp.float32)
        v_block = lax.dynamic_slice_in_dim(own_value, start, block_slice, 0).astype(jnp.float32)
        chosen_prefix = lax.dynamic_slice_in_dim(prefix_of[:, 0], start, block_slice, 0)
        limit = lax.dynamic_slice_in_dim(positions, start, block_slice, 0)
        key_rows = jnp.take(rotated_prefix_keys, chosen_prefix, axis=0).reshape(block_slice, PREFIX_LENGTH, KEY_VALUE_HEADS, HEAD_SIZE).astype(jnp.float32)
        value_rows = jnp.take(shared_prefix_values, chosen_prefix, axis=0).reshape(block_slice, PREFIX_LENGTH, KEY_VALUE_HEADS, HEAD_SIZE).astype(jnp.float32)
        far = jnp.einsum("bskgd,blkd->bskgl", q_block, key_rows) * scale
        allowed = jnp.arange(PREFIX_LENGTH, dtype=jnp.int32)[None, :] < limit[:, None]
        far = jnp.where(allowed[:, None, None, None, :], far, -1e30)
        near = jnp.einsum("bskgd,btkd->bskgt", q_block, k_block) * scale
        causal = jnp.arange(DECODE_STEPS)[:, None] >= jnp.arange(DECODE_STEPS)[None, :]
        near = jnp.where(causal[None, :, None, None, :], near, -1e30)
        top = jnp.maximum(jnp.max(far, axis=-1), jnp.max(near, axis=-1))
        far_w = jnp.exp(far - top[..., None])
        near_w = jnp.exp(near - top[..., None])
        total = jnp.sum(far_w, axis=-1) + jnp.sum(near_w, axis=-1)
        far_b = lax.optimization_barrier(far_w.astype(jnp.bfloat16)).astype(jnp.float32)
        near_b = lax.optimization_barrier(near_w.astype(jnp.bfloat16)).astype(jnp.float32)
        summed = jnp.einsum("bskgl,blkd->bskgd", far_b, value_rows) + jnp.einsum("bskgt,btkd->bskgd", near_b, v_block)
        result = summed / total[..., None]
        return result.astype(jnp.bfloat16).reshape(block_slice, DECODE_STEPS, QUERY_HEADS * HEAD_SIZE)

    pieces = lax.map(attend, jnp.arange(REQUEST_COUNT // block_slice, dtype=jnp.int32))
    return pieces.reshape(REQUEST_COUNT, DECODE_STEPS, QUERY_HEADS * HEAD_SIZE)
```

```python
import functools
import math

import jax
import jax.numpy as jnp
from jax import lax
from jax.experimental import pallas as pl
from jax.experimental.pallas import tpu as pltpu
from jax.sharding import PartitionSpec as P

HEAD = 128
STEPS = 2
XS = 4
MESH = pl.DeviceIdType.MESH
BF = jnp.bfloat16
F32 = jnp.float32
I32 = jnp.int32
HI = lax.Precision.HIGHEST


def iota(shape, dim):
    return lax.broadcasted_iota(I32, shape, dim)


def to_column(row, n):
    eye = iota((n, row.shape[1]), 0) == iota((n, row.shape[1]), 1)
    return jnp.sum(jnp.where(eye, row, 0), axis=1, keepdims=True)


def frequencies():
    lane = iota((1, HEAD), 1) % (HEAD // 2)
    high, low = lane // 8, lane % 8
    a = jnp.full((1, HEAD), 1.0, F32)
    b = jnp.full((1, HEAD), 1.0, F32)
    for t in range(1, 8):
        a = jnp.where(high == t, 10000.0 ** (-8 * t / 64), a)
        b = jnp.where(low == t, 10000.0 ** (-t / 64), b)
    return a * b


def kernel(
    dims,
    tok,
    w,
    keys,
    vals,
    pref,
    pos,
    out,
    wbuf,
    tokbuf,
    kbuf,
    vbuf,
    meta,
    metabuf,
    cosbuf,
    sinbuf,
    limsend,
    limrecv,
    hsend,
    hrecv,
    qsend,
    qrecv,
    fsend,
    frecv,
    lsend,
    lrecv,
    wxs,
    wxr,
    zs,
    zr,
    ps,
    pr,
    t1s,
    t1r,
    m1s,
    m1r,
    ys,
    yr,
    kvs,
    hs,
    hr,
    ais,
    air,
    loc,
):
    zn, yn = dims
    pn = XS * zn
    t_rows = tok.shape[0]
    reqs = t_rows // STEPS
    wide, nar = lax.axis_index("wide"), lax.axis_index("narrow")
    x, z = wide // zn, wide % zn
    y, c = nar // 2, nar % 2
    k, jx = x // 2, x % 2
    selfcase = k == c

    def dev(xx, zz, yy, cc):
        return {"wide": xx * zn + zz, "narrow": yy * 2 + cc}

    def remote(src, dst, ss, rs, where):
        return pltpu.make_async_remote_copy(
            src_ref=src, dst_ref=dst, send_sem=ss, recv_sem=rs, device_id=where, device_id_type=MESH
        )

    def took(ref, sem):
        pltpu.make_async_copy(ref, ref, sem).wait()

    up_z, down_z = (z + 1) % zn, (z + zn - 1) % zn
    up_y, down_y = (y + 1) % yn, (y + yn - 1) % yn

    barrier = pltpu.get_barrier_semaphore()
    peers = [dev((x + o) % XS, z, y, (c + d) % 2) for o in range(XS) for d in range(2) if o or d]
    if zn > 1:
        peers += [dev(x, up_z, y, c), dev(x, down_z, y, c)]
    if yn > 1:
        peers += [dev(x, z, up_y, c), dev(x, z, down_y, c)]
    for peer in peers:
        pl.semaphore_signal(barrier, inc=1, device_id=peer, device_id_type=MESH)

    kcopy = pltpu.make_async_copy(keys.at[0], kbuf, kvs.at[0])
    vcopy = pltpu.make_async_copy(vals.at[0], vbuf, kvs.at[1])
    kcopy.start()
    vcopy.start()

    pcol = to_column(pref[...], reqs)
    before = (pcol == pref[...]) & (iota((reqs, reqs), 0) < iota((reqs, reqs), 1))
    rank = jnp.sum(before.astype(I32), axis=0, keepdims=True)
    code_col = to_column(pref[...] * 8 + rank * 2, reqs)
    pos_col = to_column(pos[...], reqs)
    spread = iota((reqs, t_rows), 0) == iota((reqs, t_rows), 1) % reqs
    step_lane = iota((1, t_rows), 1) // reqs
    code_row = jnp.sum(jnp.where(spread, code_col, 0), axis=0, keepdims=True) + step_lane
    place_row = jnp.sum(jnp.where(spread, pos_col, 0), axis=0, keepdims=True) + step_lane
    which = iota((8, t_rows), 0)
    meta[...] = jnp.where(which == 0, code_row, jnp.where(which == 1, place_row, 0))

    pl.semaphore_wait(barrier, len(peers))

    def wx(j, part):
        if part == 0:
            src = w.at[:, pl.ds(2 * HEAD * j, 2 * HEAD)]
            dst = wbuf.at[wide, :, pl.ds(0, 2 * HEAD)]
        else:
            src = w.at[:, pl.ds(4 * HEAD + HEAD * j, HEAD)]
            dst = wbuf.at[wide, :, pl.ds(2 * HEAD, HEAD)]
        rsem = wxr.at[jx, part]
        return (
            remote(src, dst, wxs.at[j, part], rsem, dev(2 * c + j, z, y, k)),
            pltpu.make_async_copy(src, dst, rsem),
        )

    def either(pair, is_self):
        @pl.when(is_self)
        def _():
            pair[1].start()

        @pl.when(jnp.logical_not(is_self))
        def _():
            pair[0].start()

    def sent(pair, is_self):
        @pl.when(jnp.logical_not(is_self))
        def _():
            pair[0].wait_send()

    for j in range(2):
        for part in range(2):
            either(wx(j, part), selfcase & (jx == j))

    def tok1(o):
        target = dev((x + o) % XS, z, y, k)
        src, dst, rsem = tok, tokbuf.at[nar, jx], t1r.at[c, jx]
        return remote(src, dst, t1s.at[o], rsem, target), pltpu.make_async_copy(src, dst, rsem)

    def met1(o):
        target = dev((x + o) % XS, z, y, k)
        src, dst, rsem = meta, metabuf.at[c, jx], m1r.at[c, jx]
        return remote(src, dst, m1s.at[o], rsem, target), pltpu.make_async_copy(src, dst, rsem)

    for o in range(XS):
        either(tok1(o), selfcase if o == 0 else jnp.bool_(False)) if o == 0 else tok1(o)[0].start()
    for o in range(XS):
        either(met1(o), selfcase) if o == 0 else met1(o)[0].start()

    def reach(n):
        return {(0, 0): n // 2, (0, 1): (n - 1) // 2, (1, 0): (n - 1) // 2, (1, 1): n // 2}

    zreach, yreach = reach(zn), reach(yn)
    zto = (up_z, down_z)
    yto = (up_y, down_y)

    def zsend(direction, i, d):
        origin = (z + zn - d) % zn if direction == 0 else (z + d) % zn
        slot = (2 * c + i) * zn + origin
        remote(
            wbuf.at[slot], wbuf.at[slot], zs, zr.at[direction, i, d], dev(x, zto[direction], y, c)
        ).start()

    def partner(i, origin):
        slot = (2 * c + i) * zn + origin
        remote(wbuf.at[slot], wbuf.at[slot], ps, pr, dev(x, z, y, 1 - c)).start()

    def ysend(direction, i, cc, d):
        origin = (y + yn - d) % yn if direction == 0 else (y + d) % yn
        slot = origin * 2 + cc
        remote(
            tokbuf.at[slot, i],
            tokbuf.at[slot, i],
            ys,
            yr.at[direction, i, cc, d],
            dev(x, z, yto[direction], c),
        ).start()

    for i in range(2):
        slot = (2 * c + i) * zn + z
        took(wbuf.at[slot, :, pl.ds(0, 2 * HEAD)], wxr.at[i, 0])
        took(wbuf.at[slot, :, pl.ds(2 * HEAD, HEAD)], wxr.at[i, 1])
        for direction in range(2):
            if zreach[direction, i] > 0:
                zsend(direction, i, 0)
        partner(i, z)

    for i in range(2):
        for cc in range(2):
            took(tokbuf.at[y * 2 + cc, i], t1r.at[cc, i])
            for direction in range(2):
                if yreach[direction, i] > 0:
                    ysend(direction, i, cc, 0)

    def angles():
        freq = frequencies()
        for i in range(2):
            for cc in range(2):
                took(metabuf.at[cc, i], m1r.at[cc, i])
            place = to_column(metabuf[0, i, 1:2, :], t_rows).astype(F32)
            angle = place * freq
            low = iota((t_rows, HEAD), 1) < HEAD // 2
            sine = jnp.sin(angle)
            cosbuf[i] = jnp.cos(angle)
            sinbuf[i] = jnp.where(low, -sine, sine)

    def ystep(d):
        for i in range(2):
            for direction in range(2):
                if d <= yreach[direction, i]:
                    origin = (y + yn - d) % yn if direction == 0 else (y + d) % yn
                    for cc in range(2):
                        took(tokbuf.at[origin * 2 + cc, i], yr.at[direction, i, cc, d - 1])
                        if d < yreach[direction, i]:
                            ysend(direction, i, cc, d)

    ysteps = yn // 2
    ydone = 0
    for d in range(1, zn // 2 + 1):
        for i in range(2):
            for direction in range(2):
                if d <= zreach[direction, i]:
                    origin = (z + zn - d) % zn if direction == 0 else (z + d) % zn
                    slot = (2 * c + i) * zn + origin
                    took(wbuf.at[slot], zr.at[direction, i, d - 1])
                    if d < zreach[direction, i]:
                        zsend(direction, i, d)
                    partner(i, origin)
        if d == 1:
            angles()
        if ydone < ysteps - 1 and d == min(4, zn // 2):
            ydone += 1
            ystep(ydone)
    while ydone < ysteps:
        ydone += 1
        ystep(ydone)
    if zn < 2:
        angles()

    lane = iota((reqs, HEAD), 1)
    halves = jnp.where(lane < 4, pos_col // 64, pos_col % 64).astype(F32).astype(BF)
    code64 = pref[...] * 8 + rank * 2
    prow = iota((pn, reqs), 0) * 8
    lim = [
        jnp.dot(
            (code64 == prow + 2 * u).astype(F32).astype(BF), halves, preferred_element_type=F32
        )
        for u in range(2)
    ]
    limits = jnp.where((iota((pn, HEAD), 1) // 2) % 2 == 0, lim[0], lim[1])
    limsend[...] = limits.reshape(pn, 1, HEAD)

    took(wbuf.at[pl.ds(0, 2 * zn)], pr)

    def each_wide(fn):
        def step(o, carry):
            fn((wide + o) % pn)
            return carry

        lax.fori_loop(1, pn, step, 0)

    def send_limit(p):
        remote(
            limsend.at[p],
            limrecv.at[z * XS + x],
            ais.at[0],
            air.at[0],
            {"wide": p, "narrow": nar},
        ).start()

    each_wide(send_limit)
    own_limit = pltpu.make_async_copy(limsend.at[wide], limrecv.at[z * XS + x], loc.at[0])
    own_limit.start()

    nb = pn // (2 * yn)
    depth = w.shape[0]
    acc = None
    for n in range(2 * yn):
        left = tokbuf[n].reshape(2 * t_rows, tok.shape[1])
        right = wbuf[n * nb : (n + 1) * nb].reshape(nb * depth, 3 * HEAD)
        part = jnp.dot(left, right, preferred_element_type=F32)
        acc = part if acc is None else acc + part
    cosine = cosbuf[...].reshape(2 * t_rows, HEAD)
    sine = sinbuf[...].reshape(2 * t_rows, HEAD)

    def rotate(v):
        return v * cosine + pltpu.roll(v, HEAD // 2, 1) * sine

    q0 = rotate(acc[:, :HEAD]).astype(BF)
    q1 = rotate(acc[:, HEAD : 2 * HEAD]).astype(BF)
    third = acc[:, 2 * HEAD :]
    third = jnp.where(jx == 0, rotate(third), third).astype(BF)

    codes = jnp.concatenate([metabuf[0, i, 0:1, :] + 4 * i for i in range(2)], axis=1)
    slots = iota((8 * pn, 2 * t_rows), 0)
    onehot = (slots == codes).astype(F32).astype(BF)
    for h, q in enumerate((q0, q1)):
        packed = jnp.dot(onehot, q, preferred_element_type=F32)
        qsend[:, :, h * HEAD : (h + 1) * HEAD] = packed.reshape(pn, 8, HEAD).astype(BF)

    def send_query(p):
        remote(
            qsend.at[p], qrecv.at[z * 2 + c, jx], ais.at[1], air.at[1], {"wide": p, "narrow": y * 2 + k}
        ).start()

    each_wide(send_query)
    own_query = pltpu.make_async_copy(qsend.at[wide], qrecv.at[z * 2 + c, jx], loc.at[1])

    @pl.when(selfcase)
    def _():
        own_query.start()

    @pl.when(jnp.logical_not(selfcase))
    def _():
        send_query(wide)

    def home(i):
        src, dst, rsem = hsend.at[i], hrecv.at[jx], hr.at[jx]
        return (
            remote(src, dst, hs.at[i], rsem, dev(2 * c + i, z, y, k)),
            pltpu.make_async_copy(src, dst, rsem),
        )

    for i in range(2):
        rows = slice(i * t_rows, (i + 1) * t_rows)
        hsend[i, :, 0:HEAD] = q0[rows]
        hsend[i, :, HEAD : 2 * HEAD] = q1[rows]
        hsend[i, :, 2 * HEAD :] = third[rows]
    for i in range(2):
        either(home(i), selfcase & (jx == i))

    kcopy.wait()
    vcopy.wait()
    took(limsend.at[pl.ds(0, pn - 1)], ais.at[0])
    took(limsend.at[pl.ds(0, pn - 1)], air.at[0])
    own_limit.wait()

    rows_all = 4 * pn
    lim_rows = limrecv[...].reshape(pn, HEAD).astype(BF)
    owner = (iota((rows_all, pn), 0) // 4 == iota((rows_all, pn), 1)).astype(F32).astype(BF)
    lim_all = jnp.dot(owner, lim_rows, preferred_element_type=F32)
    rlane, rsub = iota((rows_all, HEAD), 1), iota((rows_all, HEAD), 0) % 4
    pick = jnp.where(rlane == rsub, 64.0, jnp.where(rlane == rsub + 4, 1.0, 0.0))
    limit = jnp.sum(lim_all * pick, axis=1, keepdims=True).astype(I32)

    @pl.when(selfcase)
    def _():
        own_query.wait()
        took(qsend.at[pl.ds(0, pn - 1)], ais.at[1])
        took(qsend.at[pl.ds(0, pn - 1)], air.at[1])

    @pl.when(jnp.logical_not(selfcase))
    def _():
        took(qsend, ais.at[1])
        took(qsend, air.at[1])

    scale = 1.0 / HEAD**0.5
    length = kbuf.shape[0]
    allowed = iota((rows_all, length), 1) < limit
    lse_all = jnp.zeros((rows_all, HEAD), F32)
    low8 = iota((2 * zn, 8, HEAD), 1) < 4
    for h in range(2):
        halves_out = []
        for j in range(2):
            q = qrecv[:, j, :, h * HEAD : (h + 1) * HEAD].astype(F32)
            q = q.reshape(rows_all, HEAD).astype(BF)
            s = lax.dot_general(
                q, kbuf[...], (((1,), (1,)), ((), ())), preferred_element_type=F32
            )
            s = jnp.where(allowed, s * scale, -1e30)
            top = jnp.max(s, axis=1, keepdims=True)
            e = jnp.exp(s - top)
            total = jnp.sum(e, axis=1, keepdims=True)
            o = jnp.dot(e.astype(BF), vbuf[...], preferred_element_type=F32) / total
            lse = top + jnp.log(total)
            lse_all = jnp.where(rlane == (2 * j + h) * 4 + rsub, lse, lse_all)
            halves_out.append(o.reshape(2 * zn, 8, HEAD))
        a, b = halves_out
        ra, rb = pltpu.roll(a, 4, 1), pltpu.roll(b, 4, 1)
        fsend[0, :, :, h * HEAD : (h + 1) * HEAD] = jnp.where(low8, a, rb).astype(BF)
        fsend[1, :, :, h * HEAD : (h + 1) * HEAD] = jnp.where(low8, ra, b).astype(BF)
    gather4 = (iota((pn, rows_all), 1) // 4 == iota((pn, rows_all), 0)).astype(F32)
    lses = jnp.dot(gather4, lse_all, preferred_element_type=F32, precision=HI)
    lsend[...] = lses.reshape(pn, 1, HEAD)

    def send_result(p):
        xx, zz = p // zn, p % zn
        remote(
            fsend.at[xx % 2, zz * 2 + xx // 2],
            frecv.at[wide],
            ais.at[2],
            air.at[2],
            {"wide": p, "narrow": nar},
        ).start()
        remote(
            lsend.at[zz * XS + xx], lrecv.at[wide], ais.at[3], air.at[3], {"wide": p, "narrow": nar}
        ).start()

    each_wide(send_result)
    own_far = pltpu.make_async_copy(fsend.at[jx, z * 2 + k], frecv.at[wide], loc.at[2])
    own_lse = pltpu.make_async_copy(lsend.at[z * XS + x], lrecv.at[wide], loc.at[3])
    own_far.start()
    own_lse.start()

    for i in range(2):
        took(hrecv.at[i], hr.at[i])
    key = hrecv[0, :, 2 * HEAD :].astype(F32)
    value = hrecv[1, :, 2 * HEAD :].astype(F32)
    key_first = jnp.concatenate([key[:reqs], key[:reqs]], axis=0)
    value_first = jnp.concatenate([value[:reqs], value[:reqs]], axis=0)
    second = iota((t_rows, 1), 0) >= reqs
    same, prev = [], []
    for g in range(4):
        q = hrecv[g // 2, :, (g % 2) * HEAD : (g % 2 + 1) * HEAD].astype(F32)
        same.append(jnp.sum(q * key, axis=1, keepdims=True) * scale)
        early = jnp.sum(q * key_first, axis=1, keepdims=True) * scale
        prev.append(jnp.where(second, early, -1e30))
    code = to_column(meta[0:1, :], t_rows)

    took(fsend.at[0, pl.ds(0, pn // 2)], ais.at[2])
    took(fsend.at[0, pl.ds(0, pn // 2 - 1)], ais.at[2])
    took(frecv.at[pl.ds(0, pn - 1)], air.at[2])
    took(lsend.at[pl.ds(0, pn - 1)], ais.at[3])
    took(lrecv.at[pl.ds(0, pn - 1)], air.at[3])
    own_far.wait()
    own_lse.wait()

    far_rows = frecv[...].astype(F32).reshape(8 * pn, 2 * HEAD).astype(BF)
    lse_rows = lrecv[...].reshape(pn, HEAD)
    owner_p = (iota((t_rows, pn), 1) == code // 8).astype(F32)
    lse_mine = jnp.dot(owner_p, lse_rows, preferred_element_type=F32, precision=HI)
    slot_cols = iota((t_rows, 8 * pn), 1)
    lane = iota((t_rows, HEAD), 1)
    for j in range(2):
        pickj = (slot_cols == code + 4 * j).astype(F32).astype(BF)
        far2 = jnp.dot(pickj, far_rows, preferred_element_type=F32)
        for h in range(2):
            g = 2 * j + h
            lse = jnp.sum(
                jnp.where(lane == g * 4 + code % 8, lse_mine, 0.0), axis=1, keepdims=True
            )
            top = jnp.maximum(jnp.maximum(lse, same[g]), prev[g])
            ef, es, ep = jnp.exp(lse - top), jnp.exp(same[g] - top), jnp.exp(prev[g] - top)
            total = ef + es + ep
            num = far2[:, h * HEAD : (h + 1) * HEAD] * ef + value * es + value_first * ep
            out[:, g * HEAD : (g + 1) * HEAD] = (num / total).astype(BF)

    for j in range(2):
        for part in range(2):
            sent(wx(j, part), selfcase & (jx == j))
    for o in range(XS):
        sent(tok1(o), selfcase) if o == 0 else tok1(o)[0].wait_send()
        sent(met1(o), selfcase) if o == 0 else met1(o)[0].wait_send()
    if zn > 1:
        took(wbuf.at[pl.ds(0, 2 * (zn - 1))], zs)
    took(wbuf.at[pl.ds(0, 2 * zn)], ps)
    if yn > 1:
        took(tokbuf.at[pl.ds(0, 2 * (yn - 1))], ys)
    for i in range(2):
        sent(home(i), selfcase & (jx == i))


def on_device(dims, tokens, qkv_weight, rotated_prefix_keys, shared_prefix_values, prefix_of, positions):
    zn, yn = dims
    pn = XS * zn
    reqs, _, feat = tokens.shape
    t_rows = reqs * STEPS
    depth = qkv_weight.shape[0]
    length = rotated_prefix_keys.shape[1]
    tok = tokens.transpose(1, 0, 2).reshape(t_rows, feat)
    vm = pl.BlockSpec(memory_space=pltpu.VMEM)
    hbm = pl.BlockSpec(memory_space=pl.ANY)
    dma = pltpu.SemaphoreType.DMA
    zmax, ymax = max(1, zn // 2), max(1, yn // 2)
    V = pltpu.VMEM
    result = pl.pallas_call(
        functools.partial(kernel, dims),
        out_shape=jax.ShapeDtypeStruct((t_rows, 4 * HEAD), BF),
        in_specs=[vm, hbm, hbm, hbm, vm, vm],
        out_specs=vm,
        scratch_shapes=[
            V((pn, depth, 3 * HEAD), BF),
            V((2 * yn, 2, t_rows, feat), BF),
            V((length, HEAD), BF),
            V((length, HEAD), BF),
            V((8, t_rows), I32),
            V((2, 2, 8, t_rows), I32),
            V((2, t_rows, HEAD), F32),
            V((2, t_rows, HEAD), F32),
            V((pn, 1, HEAD), F32),
            V((pn, 1, HEAD), F32),
            V((2, t_rows, 3 * HEAD), BF),
            V((2, t_rows, 3 * HEAD), BF),
            V((pn, 8, 2 * HEAD), BF),
            V((2 * zn, 2, 8, 2 * HEAD), BF),
            V((2, 2 * zn, 8, 2 * HEAD), BF),
            V((pn, 8, 2 * HEAD), BF),
            V((pn, 1, HEAD), F32),
            V((pn, 1, HEAD), F32),
            dma((2, 2)),
            dma((2, 2)),
            dma(()),
            dma((2, 2, zmax)),
            dma(()),
            dma(()),
            dma((XS,)),
            dma((2, 2)),
            dma((XS,)),
            dma((2, 2)),
            dma(()),
            dma((2, 2, 2, ymax)),
            dma((2,)),
            dma((2,)),
            dma((2,)),
            dma((4,)),
            dma((4,)),
            dma((4,)),
        ],
        compiler_params=pltpu.CompilerParams(
            collective_id=0, has_side_effects=True, vmem_limit_bytes=60 * 2**20
        ),
        name="decode_step",
    )(
        tok,
        qkv_weight,
        rotated_prefix_keys,
        shared_prefix_values,
        prefix_of.reshape(1, reqs),
        positions.reshape(1, reqs),
    )
    return result.reshape(STEPS, reqs, 4 * HEAD).transpose(1, 0, 2)


def solution(mesh):
    dims = (mesh.shape["wide"] // XS, mesh.shape["narrow"] // 2)
    return jax.shard_map(
        functools.partial(on_device, dims),
        mesh=mesh,
        in_specs=(
            P("wide", None, "narrow"),
            P("wide", "narrow"),
            P("wide", None, "narrow"),
            P("wide", None, "narrow"),
            P("wide", None),
            P("wide"),
        ),
        out_specs=P("wide", None, "narrow"),
        check_vma=False,
    )
```

```python
import functools
import math

import jax
import jax.numpy as jnp
from jax import lax
from jax.experimental import pallas as pl
from jax.experimental.pallas import tpu as pltpu
from jax.sharding import PartitionSpec as P

HEAD = 128
STEPS = 2
XS = 4
PARTS = 3
XAT = 3
MESH = pl.DeviceIdType.MESH
BF = jnp.bfloat16
F32 = jnp.float32
I32 = jnp.int32
HI = lax.Precision.HIGHEST


def iota(shape, dim):
    return lax.broadcasted_iota(I32, shape, dim)


def to_column(row, n):
    eye = iota((n, row.shape[1]), 0) == iota((n, row.shape[1]), 1)
    return jnp.sum(jnp.where(eye, row, 0), axis=1, keepdims=True)


def frequencies():
    lane = iota((1, HEAD), 1) % (HEAD // 2)
    high, low = lane // 8, lane % 8
    a = jnp.full((1, HEAD), 1.0, F32)
    b = jnp.full((1, HEAD), 1.0, F32)
    for t in range(1, 8):
        a = jnp.where(high == t, 10000.0 ** (-8 * t / 64), a)
        b = jnp.where(low == t, 10000.0 ** (-t / 64), b)
    return a * b


def kernel(
    dims,
    traw,
    w,
    keys,
    vals,
    pref,
    pos,
    out,
    wown,
    tokin,
    tok,
    wbuf,
    tokbuf,
    kbuf,
    vbuf,
    meta,
    metabuf,
    cosbuf,
    sinbuf,
    limsend,
    limrecv,
    hsend,
    hrecv,
    qsend,
    qrecv,
    fsend,
    frecv,
    lsend,
    lrecv,
    wxs,
    wxr,
    zs,
    zr,
    ps,
    pr,
    t1s,
    t1r,
    m1s,
    m1r,
    xs,
    xr,
    xs2,
    xr2,
    kvs,
    hs,
    hr,
    qs,
    qr,
    qloc,
    fs,
    fr,
    floc,
    ais,
    air,
    loc,
):
    zn, yn = dims
    pn = XS * zn
    t_rows = tok.shape[0]
    reqs = t_rows // STEPS
    wide, nar = lax.axis_index("wide"), lax.axis_index("narrow")
    x, z = wide // zn, wide % zn
    y, c = nar // 2, nar % 2
    k, jx = x // 2, x % 2
    selfcase = k == c

    def dev(xx, zz, yy, cc):
        return {"wide": xx * zn + zz, "narrow": yy * 2 + cc}

    def remote(src, dst, ss, rs, where):
        return pltpu.make_async_remote_copy(
            src_ref=src, dst_ref=dst, send_sem=ss, recv_sem=rs, device_id=where, device_id_type=MESH
        )

    def took(ref, sem):
        pltpu.make_async_copy(ref, ref, sem).wait()

    up_z, down_z = (z + 1) % zn, (z + zn - 1) % zn

    barrier = pltpu.get_barrier_semaphore()
    peers = [dev((x + o) % XS, z, y, (c + d) % 2) for o in range(XS) for d in range(2) if o or d]
    if zn > 1:
        peers += [dev(x, up_z, y, c), dev(x, down_z, y, c)]
    if yn > 1:
        peers += [dev(x, z, (y + o) % yn, (c + d) % 2) for o in range(1, yn) for d in range(2)]
    for peer in peers:
        pl.semaphore_signal(barrier, inc=1, device_id=peer, device_id_type=MESH)

    kcopy = pltpu.make_async_copy(keys.at[0], kbuf, kvs.at[0])
    vcopy = pltpu.make_async_copy(vals.at[0], vbuf, kvs.at[1])
    kcopy.start()
    vcopy.start()

    wcopy = pltpu.make_async_copy(w, wown, loc.at[2])
    tcopy = pltpu.make_async_copy(traw, tokin, loc.at[3])
    wcopy.start()
    tcopy.start()
    wcopy.wait()
    pl.semaphore_wait(barrier, len(peers))

    def wx(j, part):
        start = 4 * HEAD + HEAD * j if part == 2 else HEAD * (2 * j + part)
        src = wown.at[:, pl.ds(start, HEAD)]
        dst = wbuf.at[part, wide]
        rsem = wxr.at[jx, part]
        return (
            lambda: remote(src, dst, wxs.at[j, part], rsem, dev(2 * c + j, z, y, k)),
            lambda: pltpu.make_async_copy(src, dst, rsem),
        )

    def either(pair, is_self):
        @pl.when(is_self)
        def _():
            pair[1]().start()

        @pl.when(jnp.logical_not(is_self))
        def _():
            pair[0]().start()

    def sent(pair, is_self):
        @pl.when(jnp.logical_not(is_self))
        def _():
            pair[0]().wait_send()

    for part in range(PARTS):
        for j in range(2):
            either(wx(j, part), selfcase & (jx == j))

    tcopy.wait()
    for step in range(STEPS):
        tok[step * reqs : (step + 1) * reqs] = tokin[:, step, :]

    def token(o):
        dst, rsem = tokbuf.at[nar, jx], t1r.at[nar]
        return (
            lambda: remote(tok, dst, t1s.at[o], rsem, dev(x, z, (y + o) % yn, k)),
            lambda: pltpu.make_async_copy(tok, dst, rsem),
        )

    yorder = [0, 1, 3, 2] if yn == 4 else list(range(yn))
    for o in yorder:
        if o:
            token(o)[0]().start()
        else:
            either(token(o), selfcase)

    pcol = to_column(pref[...], reqs)
    before = (pcol == pref[...]) & (iota((reqs, reqs), 0) < iota((reqs, reqs), 1))
    rank = jnp.sum(before.astype(I32), axis=0, keepdims=True)
    code_col = to_column(pref[...] * 8 + rank * 2, reqs)
    pos_col = to_column(pos[...], reqs)
    spread = iota((reqs, t_rows), 0) == iota((reqs, t_rows), 1) % reqs
    step_lane = iota((1, t_rows), 1) // reqs
    code_row = jnp.sum(jnp.where(spread, code_col, 0), axis=0, keepdims=True) + step_lane
    place_row = jnp.sum(jnp.where(spread, pos_col, 0), axis=0, keepdims=True) + step_lane
    which = iota((8, t_rows), 0)
    meta[...] = jnp.where(which == 0, code_row, jnp.where(which == 1, place_row, 0))


    def routes_to(o):
        dst, rsem = metabuf.at[c, jx], m1r.at[c, jx]
        return (
            lambda: remote(meta, dst, m1s.at[o], rsem, dev((x + o) % XS, z, y, k)),
            lambda: pltpu.make_async_copy(meta, dst, rsem),
        )

    for o in range(XS):
        if o:
            routes_to(o)[0]().start()
        else:
            either(routes_to(o), selfcase)

    near = jnp.where(selfcase, jx, 1 - jx)
    block = (near, 1 - near)

    def reach(n):
        return {(0, 0): n // 2, (0, 1): (n - 1) // 2, (1, 0): (n - 1) // 2, (1, 1): n // 2}

    zreach = reach(zn)
    zto = (up_z, down_z)

    def zslot(direction, a, d):
        origin = (z + zn - d) % zn if direction == 0 else (z + d) % zn
        return (2 * c + block[a]) * zn + origin

    def zsend(direction, a, part, d):
        ref = wbuf.at[part, zslot(direction, a, d)]
        remote(ref, ref, zs, zr.at[direction, a, part, d], dev(x, zto[direction], y, c)).start()

    def partner(direction, a, d):
        ref = wbuf.at[:, zslot(direction, a, d)]
        remote(ref, ref, ps, pr, dev(x, z, y, 1 - c)).start()

    order = [((y + o) % yn) * 2 + (c + cc) % 2 for o in yorder for cc in range(2)]
    plus = selfcase == (jx == 1)
    ahead = jnp.where(plus, (x + 1) % XS, (x + XS - 1) % XS)
    behind = jnp.where(plus, (x + XS - 1) % XS, (x + 1) % XS)
    onward = jnp.where(plus, 0, 1)

    def own_rows(m):
        @pl.when(selfcase)
        def _():
            ref = tokbuf.at[order[m], jx]
            took(ref, t1r.at[order[m]])
            for side in (1, XS - 1):
                remote(ref, ref, xs, xr.at[order[m]], dev((x + side) % XS, z, y, c)).start()

    def next_rows(m):
        ref = tokbuf.at[order[m], behind % 2]
        took(ref, xr.at[order[m]])

        @pl.when(order[m] % 2 == onward)
        def _():
            remote(ref, ref, xs2, xr2.at[order[m]], dev(ahead, z, y, c)).start()

    for a in range(2):
        for part in range(PARTS):
            took(wbuf.at[part, zslot(0, a, 0)], wxr.at[block[a], part])
            for direction in range(2):
                if zreach[direction, a] > 0:
                    zsend(direction, a, part, 0)
        partner(0, a, 0)
        for m in range(2):
            if 2 * a + m < 2 * yn:
                own_rows(2 * a + m)

    def angles():
        freq = frequencies()
        for i in range(2):
            for cc in range(2):
                took(metabuf.at[cc, i], m1r.at[cc, i])
            place = to_column(metabuf[0, i, 1:2, :], t_rows).astype(F32)
            angle = place * freq
            low = iota((t_rows, HEAD), 1) < HEAD // 2
            sine = jnp.sin(angle)
            cosbuf[i] = jnp.cos(angle)
            sinbuf[i] = jnp.where(low, -sine, sine)

    rest = list(range(4, 2 * yn))
    coming = list(range(2 * yn))
    for d in range(1, zn // 2 + 1):
        for part in range(PARTS):
            for a in range(2):
                for direction in range(2):
                    if d <= zreach[direction, a]:
                        took(
                            wbuf.at[part, zslot(direction, a, d)],
                            zr.at[direction, a, part, d - 1],
                        )
                        if d < zreach[direction, a]:
                            zsend(direction, a, part, d)
                        if part == PARTS - 1:
                            partner(direction, a, d)
        for m in rest[:2]:
            own_rows(m)
        rest = rest[2:]
        if d == 1:
            angles()
        if d >= XAT:
            for m in coming[:2]:
                next_rows(m)
            coming = coming[2:]
    for m in rest:
        own_rows(m)
    for m in coming:
        next_rows(m)

    @pl.when(jnp.logical_not(selfcase))
    def _():
        for m in range(2 * yn):
            took(tokbuf.at[order[m], 1 - behind % 2], xr2.at[order[m]])

    lane = iota((reqs, HEAD), 1)
    halves = jnp.where(lane < 4, pos_col // 64, pos_col % 64).astype(F32).astype(BF)
    code64 = pref[...] * 8 + rank * 2
    prow = iota((pn, reqs), 0) * 8
    lim = [
        jnp.dot(
            (code64 == prow + 2 * u).astype(F32).astype(BF), halves, preferred_element_type=F32
        )
        for u in range(2)
    ]
    limits = jnp.where((iota((pn, HEAD), 1) // 2) % 2 == 0, lim[0], lim[1])
    limsend[...] = limits.reshape(pn, 1, HEAD)

    took(wbuf.at[:, pl.ds(0, 2 * zn)], pr)

    def each_wide(fn):
        def step(o, carry):
            fn((wide + o) % pn)
            return carry

        lax.fori_loop(1, pn, step, 0)

    def send_limit(p):
        remote(
            limsend.at[p],
            limrecv.at[z * XS + x],
            ais.at[0],
            air.at[0],
            {"wide": p, "narrow": nar},
        ).start()

    each_wide(send_limit)
    own_limit = pltpu.make_async_copy(limsend.at[wide], limrecv.at[z * XS + x], loc.at[0])
    own_limit.start()

    nb = pn // (2 * yn)
    depth = w.shape[0]
    cosine = cosbuf[...].reshape(2 * t_rows, HEAD)
    sine = sinbuf[...].reshape(2 * t_rows, HEAD)

    def project(part):
        acc = None
        for n in range(2 * yn):
            left = tokbuf[n].reshape(2 * t_rows, tok.shape[1])
            right = wbuf[part, n * nb : (n + 1) * nb].reshape(nb * depth, HEAD)
            term = jnp.dot(left, right, preferred_element_type=F32)
            acc = term if acc is None else acc + term
        return acc

    def rotate(v):
        return v * cosine + pltpu.roll(v, HEAD // 2, 1) * sine

    codes = jnp.concatenate([metabuf[0, i, 0:1, :] + 4 * i for i in range(2)], axis=1)
    slots = iota((8 * pn, 2 * t_rows), 0)
    onehot = (slots == codes).astype(F32).astype(BF)
    for h in range(2):
        q = rotate(project(h)).astype(BF)
        packed = jnp.dot(onehot, q, preferred_element_type=F32)
        qsend[h] = packed.reshape(pn, 8, HEAD).astype(BF)

        def send_query(p, h=h):
            remote(
                qsend.at[h, p],
                qrecv.at[h, z * 2 + c, jx],
                qs.at[h],
                qr.at[h],
                {"wide": p, "narrow": y * 2 + k},
            ).start()

        each_wide(send_query)

        @pl.when(selfcase)
        def _():
            pltpu.make_async_copy(qsend.at[h, wide], qrecv.at[h, z * 2 + c, jx], qloc.at[h]).start()

        @pl.when(jnp.logical_not(selfcase))
        def _():
            send_query(wide)

        for i in range(2):
            hsend[i, :, h * HEAD : (h + 1) * HEAD] = q[i * t_rows : (i + 1) * t_rows]

    third = project(2)
    third = jnp.where(jx == 0, rotate(third), third).astype(BF)
    for i in range(2):
        hsend[i, :, 2 * HEAD :] = third[i * t_rows : (i + 1) * t_rows]

    def home(i):
        src, dst, rsem = hsend.at[i], hrecv.at[jx], hr.at[jx]
        return (
            lambda: remote(src, dst, hs.at[i], rsem, dev(2 * c + i, z, y, k)),
            lambda: pltpu.make_async_copy(src, dst, rsem),
        )

    for i in range(2):
        either(home(i), selfcase & (jx == i))

    kcopy.wait()
    vcopy.wait()
    took(limsend.at[pl.ds(0, pn - 1)], ais.at[0])
    took(limsend.at[pl.ds(0, pn - 1)], air.at[0])
    own_limit.wait()

    rows_all = 4 * pn
    lim_rows = limrecv[...].reshape(pn, HEAD).astype(BF)
    owner = (iota((rows_all, pn), 0) // 4 == iota((rows_all, pn), 1)).astype(F32).astype(BF)
    lim_all = jnp.dot(owner, lim_rows, preferred_element_type=F32)
    rlane, rsub = iota((rows_all, HEAD), 1), iota((rows_all, HEAD), 0) % 4
    pick = jnp.where(rlane == rsub, 64.0, jnp.where(rlane == rsub + 4, 1.0, 0.0))
    limit = jnp.sum(lim_all * pick, axis=1, keepdims=True).astype(I32)

    scale = 1.0 / HEAD**0.5
    length = kbuf.shape[0]
    allowed = iota((rows_all, length), 1) < limit
    lse_all = jnp.zeros((rows_all, HEAD), F32)
    low8 = iota((2 * zn, 8, HEAD), 1) < 4
    gather4 = (iota((pn, rows_all), 1) // 4 == iota((pn, rows_all), 0)).astype(F32)

    def own_result(h):
        return pltpu.make_async_copy(fsend.at[h, jx, z * 2 + k], frecv.at[h, wide], floc.at[h])

    own_lse = pltpu.make_async_copy(lsend.at[z * XS + x], lrecv.at[wide], loc.at[1])
    for h in range(2):

        @pl.when(selfcase)
        def _():
            pltpu.make_async_copy(qsend.at[h, wide], qrecv.at[h, z * 2 + c, jx], qloc.at[h]).wait()
            took(qsend.at[h, pl.ds(0, pn - 1)], qs.at[h])
            took(qsend.at[h, pl.ds(0, pn - 1)], qr.at[h])

        @pl.when(jnp.logical_not(selfcase))
        def _():
            took(qsend.at[h], qs.at[h])
            took(qsend.at[h], qr.at[h])

        halves_out = []
        for j in range(2):
            q = qrecv[h, :, j].astype(F32).reshape(rows_all, HEAD).astype(BF)
            s = lax.dot_general(
                q, kbuf[...], (((1,), (1,)), ((), ())), preferred_element_type=F32
            )
            s = jnp.where(allowed, s * scale, -1e30)
            top = jnp.max(s, axis=1, keepdims=True)
            e = jnp.exp(s - top)
            total = jnp.sum(e, axis=1, keepdims=True)
            o = jnp.dot(e.astype(BF), vbuf[...], preferred_element_type=F32) / total
            lse = top + jnp.log(total)
            lse_all = jnp.where(rlane == (2 * j + h) * 4 + rsub, lse, lse_all)
            halves_out.append(o.reshape(2 * zn, 8, HEAD))
        a, b = halves_out
        ra, rb = pltpu.roll(a, 4, 1), pltpu.roll(b, 4, 1)
        fsend[h, 0] = jnp.where(low8, a, rb).astype(BF)
        fsend[h, 1] = jnp.where(low8, ra, b).astype(BF)
        if h == 1:
            lses = jnp.dot(gather4, lse_all, preferred_element_type=F32, precision=HI)
            lsend[...] = lses.reshape(pn, 1, HEAD)

        def send_result(p, h=h):
            xx, zz = p // zn, p % zn
            where = {"wide": p, "narrow": nar}
            if h == 1:
                remote(lsend.at[zz * XS + xx], lrecv.at[wide], ais.at[1], air.at[1], where).start()
            remote(
                fsend.at[h, xx % 2, zz * 2 + xx // 2], frecv.at[h, wide], fs.at[h], fr.at[h], where
            ).start()

        each_wide(send_result)
        own_result(h).start()
    own_lse.start()

    for i in range(2):
        took(hrecv.at[i], hr.at[i])
    key = hrecv[0, :, 2 * HEAD :].astype(F32)
    value = hrecv[1, :, 2 * HEAD :].astype(F32)
    key_first = jnp.concatenate([key[:reqs], key[:reqs]], axis=0)
    value_first = jnp.concatenate([value[:reqs], value[:reqs]], axis=0)
    second = iota((t_rows, 1), 0) >= reqs
    same, prev = [], []
    for g in range(4):
        q = hrecv[g // 2, :, (g % 2) * HEAD : (g % 2 + 1) * HEAD].astype(F32)
        same.append(jnp.sum(q * key, axis=1, keepdims=True) * scale)
        early = jnp.sum(q * key_first, axis=1, keepdims=True) * scale
        prev.append(jnp.where(second, early, -1e30))
    code = to_column(meta[0:1, :], t_rows)

    for h in range(2):
        took(frecv.at[h, pl.ds(0, pn - 1)], fs.at[h])
        took(frecv.at[h, pl.ds(0, pn - 1)], fr.at[h])
        own_result(h).wait()
    took(lsend.at[pl.ds(0, pn - 1)], ais.at[1])
    took(lrecv.at[pl.ds(0, pn - 1)], air.at[1])
    own_lse.wait()

    far_rows = [frecv[h].astype(F32).reshape(8 * pn, HEAD).astype(BF) for h in range(2)]
    lse_rows = lrecv[...].reshape(pn, HEAD)
    owner_p = (iota((t_rows, pn), 1) == code // 8).astype(F32)
    lse_mine = jnp.dot(owner_p, lse_rows, preferred_element_type=F32, precision=HI)
    slot_cols = iota((t_rows, 8 * pn), 1)
    lane = iota((t_rows, HEAD), 1)
    for j in range(2):
        pickj = (slot_cols == code + 4 * j).astype(F32).astype(BF)
        for h in range(2):
            far = jnp.dot(pickj, far_rows[h], preferred_element_type=F32)
            g = 2 * j + h
            lse = jnp.sum(
                jnp.where(lane == g * 4 + code % 8, lse_mine, 0.0), axis=1, keepdims=True
            )
            top = jnp.maximum(jnp.maximum(lse, same[g]), prev[g])
            ef, es, ep = jnp.exp(lse - top), jnp.exp(same[g] - top), jnp.exp(prev[g] - top)
            total = ef + es + ep
            num = far * ef + value * es + value_first * ep
            out[:, g * HEAD : (g + 1) * HEAD] = (num / total).astype(BF)

    for j in range(2):
        for part in range(PARTS):
            sent(wx(j, part), selfcase & (jx == j))
    for o in range(XS):
        if o:
            routes_to(o)[0]().wait_send()
        else:
            sent(routes_to(o), selfcase)
    for o in yorder:
        if o:
            token(o)[0]().wait_send()
        else:
            sent(token(o), selfcase)

    @pl.when(selfcase)
    def _():
        took(tokbuf, xs)

    took(tokbuf.at[pl.ds(0, yn), 0], xs2)
    if zn > 1:
        took(wbuf.at[:, pl.ds(0, 2 * (zn - 1))], zs)
    took(wbuf.at[:, pl.ds(0, 2 * zn)], ps)
    for i in range(2):
        sent(home(i), selfcase & (jx == i))


def on_device(dims, tokens, qkv_weight, rotated_prefix_keys, shared_prefix_values, prefix_of, positions):
    zn, yn = dims
    pn = XS * zn
    reqs, _, feat = tokens.shape
    t_rows = reqs * STEPS
    depth = qkv_weight.shape[0]
    length = rotated_prefix_keys.shape[1]
    vm = pl.BlockSpec(memory_space=pltpu.VMEM)
    hbm = pl.BlockSpec(memory_space=pl.ANY)
    dma = pltpu.SemaphoreType.DMA
    zmax = max(1, zn // 2)
    V = pltpu.VMEM
    result = pl.pallas_call(
        functools.partial(kernel, dims),
        out_shape=jax.ShapeDtypeStruct((t_rows, 4 * HEAD), BF),
        in_specs=[hbm, hbm, hbm, hbm, vm, vm],
        out_specs=vm,
        scratch_shapes=[
            V((depth, 6 * HEAD), BF),
            V((reqs, STEPS, feat), BF),
            V((t_rows, feat), BF),
            V((PARTS, pn, depth, HEAD), BF),
            V((2 * yn, 2, t_rows, feat), BF),
            V((length, HEAD), BF),
            V((length, HEAD), BF),
            V((8, t_rows), I32),
            V((2, 2, 8, t_rows), I32),
            V((2, t_rows, HEAD), F32),
            V((2, t_rows, HEAD), F32),
            V((pn, 1, HEAD), F32),
            V((pn, 1, HEAD), F32),
            V((2, t_rows, 3 * HEAD), BF),
            V((2, t_rows, 3 * HEAD), BF),
            V((2, pn, 8, HEAD), BF),
            V((2, 2 * zn, 2, 8, HEAD), BF),
            V((2, 2, 2 * zn, 8, HEAD), BF),
            V((2, pn, 8, HEAD), BF),
            V((pn, 1, HEAD), F32),
            V((pn, 1, HEAD), F32),
            dma((2, PARTS)),
            dma((2, PARTS)),
            dma(()),
            dma((2, 2, PARTS, zmax)),
            dma(()),
            dma(()),
            dma((yn,)),
            dma((2 * yn,)),
            dma((XS,)),
            dma((2, 2)),
            dma(()),
            dma((2 * yn,)),
            dma(()),
            dma((2 * yn,)),
            *[dma((2,)) for _ in range(11)],
            dma((4,)),
        ],
        compiler_params=pltpu.CompilerParams(
            collective_id=0, has_side_effects=True, vmem_limit_bytes=60 * 2**20
        ),
        name="decode_step",
    )(
        tokens,
        qkv_weight,
        rotated_prefix_keys,
        shared_prefix_values,
        prefix_of.reshape(1, reqs),
        positions.reshape(1, reqs),
    )
    return result.reshape(STEPS, reqs, 4 * HEAD).transpose(1, 0, 2)


def solution(mesh):
    dims = (mesh.shape["wide"] // XS, mesh.shape["narrow"] // 2)
    return jax.shard_map(
        functools.partial(on_device, dims),
        mesh=mesh,
        in_specs=(
            P("wide", None, "narrow"),
            P("wide", "narrow"),
            P("wide", None, "narrow"),
            P("wide", None, "narrow"),
            P("wide", None),
            P("wide"),
        ),
        out_specs=P("wide", None, "narrow"),
        check_vma=False,
    )
```

```python
import functools
import math

import jax
import jax.numpy as jnp
from jax import lax
from jax.experimental import pallas as pl
from jax.experimental.pallas import tpu as pltpu
from jax.sharding import PartitionSpec as P

HEAD = 128
STEPS = 2
XS = 4
PARTS = 3
XAT = 3
MESH = pl.DeviceIdType.MESH
BF = jnp.bfloat16
F32 = jnp.float32
I32 = jnp.int32
HI = lax.Precision.HIGHEST


def iota(shape, dim):
    return lax.broadcasted_iota(I32, shape, dim)


def to_column(row, n):
    eye = iota((n, row.shape[1]), 0) == iota((n, row.shape[1]), 1)
    return jnp.sum(jnp.where(eye, row, 0), axis=1, keepdims=True)


def frequencies():
    lane = iota((1, HEAD), 1) % (HEAD // 2)
    high, low = lane // 8, lane % 8
    a = jnp.full((1, HEAD), 1.0, F32)
    b = jnp.full((1, HEAD), 1.0, F32)
    for t in range(1, 8):
        a = jnp.where(high == t, 10000.0 ** (-8 * t / 64), a)
        b = jnp.where(low == t, 10000.0 ** (-t / 64), b)
    return a * b


def kernel(
    dims,
    traw,
    w,
    keys,
    vals,
    pref,
    pos,
    out,
    wown,
    tokin,
    tok,
    wbuf,
    tokbuf,
    kbuf,
    vbuf,
    meta,
    metabuf,
    cosbuf,
    sinbuf,
    limsend,
    limrecv,
    hsend,
    hrecv,
    qsend,
    qrecv,
    fsend,
    frecv,
    lsend,
    lrecv,
    wxs,
    wxr,
    zs,
    zr,
    ps,
    pr,
    t1s,
    t1r,
    m1s,
    m1r,
    xs,
    xr,
    xs2,
    xr2,
    kvs,
    hs,
    hr,
    qs,
    qr,
    qloc,
    fs,
    fr,
    floc,
    ais,
    air,
    loc,
):
    zn, yn = dims
    pn = XS * zn
    t_rows = tok.shape[0]
    reqs = t_rows // STEPS
    wide, nar = lax.axis_index("wide"), lax.axis_index("narrow")
    x, z = wide // zn, wide % zn
    y, c = nar // 2, nar % 2
    k, jx = x // 2, x % 2
    selfcase = k == c

    def dev(xx, zz, yy, cc):
        return {"wide": xx * zn + zz, "narrow": yy * 2 + cc}

    def remote(src, dst, ss, rs, where):
        return pltpu.make_async_remote_copy(
            src_ref=src, dst_ref=dst, send_sem=ss, recv_sem=rs, device_id=where, device_id_type=MESH
        )

    def took(ref, sem):
        pltpu.make_async_copy(ref, ref, sem).wait()

    up_z, down_z = (z + 1) % zn, (z + zn - 1) % zn

    barrier = pltpu.get_barrier_semaphore()
    peers = [dev((x + o) % XS, z, y, (c + d) % 2) for o in range(XS) for d in range(2) if o or d]
    if zn > 1:
        peers += [dev(x, up_z, y, c), dev(x, down_z, y, c)]
    if yn > 1:
        peers += [dev(x, z, (y + o) % yn, (c + d) % 2) for o in range(1, yn) for d in range(2)]
    for peer in peers:
        pl.semaphore_signal(barrier, inc=1, device_id=peer, device_id_type=MESH)

    kcopy = pltpu.make_async_copy(keys.at[0], kbuf, kvs.at[0])
    vcopy = pltpu.make_async_copy(vals.at[0], vbuf, kvs.at[1])
    kcopy.start()
    vcopy.start()

    wcopy = pltpu.make_async_copy(w, wown, loc.at[2])
    tcopy = pltpu.make_async_copy(traw, tokin, loc.at[3])
    wcopy.start()
    tcopy.start()
    wcopy.wait()
    pl.semaphore_wait(barrier, len(peers))

    def wx(j, part):
        start = 4 * HEAD + HEAD * j if part == 2 else HEAD * (2 * j + part)
        src = wown.at[:, pl.ds(start, HEAD)]
        dst = wbuf.at[part, wide]
        rsem = wxr.at[jx, part]
        return (
            lambda: remote(src, dst, wxs.at[j, part], rsem, dev(2 * c + j, z, y, k)),
            lambda: pltpu.make_async_copy(src, dst, rsem),
        )

    def either(pair, is_self):
        @pl.when(is_self)
        def _():
            pair[1]().start()

        @pl.when(jnp.logical_not(is_self))
        def _():
            pair[0]().start()

    def sent(pair, is_self):
        @pl.when(jnp.logical_not(is_self))
        def _():
            pair[0]().wait_send()

    for part in range(PARTS):
        for j in range(2):
            either(wx(j, part), selfcase & (jx == j))

    tcopy.wait()
    for step in range(STEPS):
        tok[step * reqs : (step + 1) * reqs] = tokin[:, step, :]

    def token(o):
        dst, rsem = tokbuf.at[nar, jx], t1r.at[nar]
        return (
            lambda: remote(tok, dst, t1s.at[o], rsem, dev(x, z, (y + o) % yn, k)),
            lambda: pltpu.make_async_copy(tok, dst, rsem),
        )

    yorder = [0, 1, 3, 2] if yn == 4 else list(range(yn))
    for o in yorder:
        if o:
            token(o)[0]().start()
        else:
            either(token(o), selfcase)

    pcol = to_column(pref[...], reqs)
    before = (pcol == pref[...]) & (iota((reqs, reqs), 0) < iota((reqs, reqs), 1))
    rank = jnp.sum(before.astype(I32), axis=0, keepdims=True)
    code_col = to_column(pref[...] * 8 + rank * 2, reqs)
    pos_col = to_column(pos[...], reqs)
    spread = iota((reqs, t_rows), 0) == iota((reqs, t_rows), 1) % reqs
    step_lane = iota((1, t_rows), 1) // reqs
    code_row = jnp.sum(jnp.where(spread, code_col, 0), axis=0, keepdims=True) + step_lane
    place_row = jnp.sum(jnp.where(spread, pos_col, 0), axis=0, keepdims=True) + step_lane
    which = iota((8, t_rows), 0)
    meta[...] = jnp.where(which == 0, code_row, jnp.where(which == 1, place_row, 0))


    def routes_to(o):
        dst, rsem = metabuf.at[c, jx], m1r.at[c, jx]
        return (
            lambda: remote(meta, dst, m1s.at[o], rsem, dev((x + o) % XS, z, y, k)),
            lambda: pltpu.make_async_copy(meta, dst, rsem),
        )

    for o in range(XS):
        if o:
            routes_to(o)[0]().start()
        else:
            either(routes_to(o), selfcase)

    lane = iota((reqs, HEAD), 1)
    halves = jnp.where(lane < 4, pos_col // 64, pos_col % 64).astype(F32).astype(BF)
    code64 = pref[...] * 8 + rank * 2
    prow = iota((pn, reqs), 0) * 8
    lim = [
        jnp.dot(
            (code64 == prow + 2 * u).astype(F32).astype(BF), halves, preferred_element_type=F32
        )
        for u in range(2)
    ]
    limits = jnp.where((iota((pn, HEAD), 1) // 2) % 2 == 0, lim[0], lim[1])
    limsend[...] = limits.reshape(pn, 1, HEAD)

    def send_limit(xx, zz):
        remote(
            limsend.at[xx * zn + zz],
            limrecv.at[z * XS + x],
            ais.at[0],
            air.at[0],
            dev(xx, zz, y, c),
        ).start()

    own_limit = pltpu.make_async_copy(limsend.at[wide], limrecv.at[z * XS + x], loc.at[0])
    own_limit.start()
    for o in range(1, XS):
        send_limit((x + o) % XS, z)

    near = jnp.where(selfcase, jx, 1 - jx)
    block = (near, 1 - near)

    def reach(n):
        return {(0, 0): n // 2, (0, 1): (n - 1) // 2, (1, 0): (n - 1) // 2, (1, 1): n // 2}

    zreach = reach(zn)
    zto = (up_z, down_z)

    def zslot(direction, a, d):
        origin = (z + zn - d) % zn if direction == 0 else (z + d) % zn
        return (2 * c + block[a]) * zn + origin

    def zsend(direction, a, part, d):
        ref = wbuf.at[part, zslot(direction, a, d)]
        remote(ref, ref, zs, zr.at[direction, a, part, d], dev(x, zto[direction], y, c)).start()

    def partner(direction, a, part, d):
        ref = wbuf.at[part, zslot(direction, a, d)]
        remote(ref, ref, ps, pr.at[part], dev(x, z, y, 1 - c)).start()

    order = [((y + o) % yn) * 2 + (c + cc) % 2 for o in yorder for cc in range(2)]
    plus = selfcase == (jx == 1)
    ahead = jnp.where(plus, (x + 1) % XS, (x + XS - 1) % XS)
    behind = jnp.where(plus, (x + XS - 1) % XS, (x + 1) % XS)
    onward = jnp.where(plus, 0, 1)

    def own_rows(m):
        @pl.when(selfcase)
        def _():
            ref = tokbuf.at[order[m], jx]
            took(ref, t1r.at[order[m]])
            for side in (1, XS - 1):
                remote(ref, ref, xs, xr.at[order[m]], dev((x + side) % XS, z, y, c)).start()

    def next_rows(m):
        ref = tokbuf.at[order[m], behind % 2]
        took(ref, xr.at[order[m]])

        @pl.when(order[m] % 2 == onward)
        def _():
            remote(ref, ref, xs2, xr2.at[order[m]], dev(ahead, z, y, c)).start()

    for a in range(2):
        for part in range(PARTS):
            took(wbuf.at[part, zslot(0, a, 0)], wxr.at[block[a], part])
            for direction in range(2):
                if zreach[direction, a] > 0:
                    zsend(direction, a, part, 0)
            partner(0, a, part, 0)
        for m in range(2):
            if 2 * a + m < 2 * yn:
                own_rows(2 * a + m)

    def angles():
        freq = frequencies()
        for i in range(2):
            for cc in range(2):
                took(metabuf.at[cc, i], m1r.at[cc, i])
            place = to_column(metabuf[0, i, 1:2, :], t_rows).astype(F32)
            angle = place * freq
            low = iota((t_rows, HEAD), 1) < HEAD // 2
            sine = jnp.sin(angle)
            cosbuf[i] = jnp.cos(angle)
            sinbuf[i] = jnp.where(low, -sine, sine)

    rest = list(range(4, 2 * yn))
    coming = list(range(2 * yn))

    def ring(d, part):
        for a in range(2):
            for direction in range(2):
                if d <= zreach[direction, a]:
                    took(
                        wbuf.at[part, zslot(direction, a, d)],
                        zr.at[direction, a, part, d - 1],
                    )
                    if d < zreach[direction, a]:
                        zsend(direction, a, part, d)
                    partner(direction, a, part, d)

    last = zn // 2
    for d in range(1, last + 1):
        for part in range(PARTS):
            if d < last or part == 0:
                ring(d, part)
        for o in range(XS):
            send_limit((x + o) % XS, (z + zn - d) % zn)
            if d <= (zn - 1) // 2:
                send_limit((x + o) % XS, (z + d) % zn)
        for m in rest[:2]:
            own_rows(m)
        rest = rest[2:]
        if d == 1:
            angles()
        if d >= XAT:
            for m in coming[:2]:
                next_rows(m)
            coming = coming[2:]
    for m in rest:
        own_rows(m)
    for m in coming:
        next_rows(m)

    @pl.when(jnp.logical_not(selfcase))
    def _():
        for m in range(2 * yn):
            took(tokbuf.at[order[m], 1 - behind % 2], xr2.at[order[m]])

    def each_wide(fn):
        half = zn // 2

        def step(t, carry):
            lap = t // XS
            away = half - (lap + 1) // 2
            dz = jnp.where(lap % 2 == 1, away, (zn - away) % zn)
            fn(((x + t + 1) % XS) * zn + (z + dz) % zn)
            return carry

        lax.fori_loop(0, pn - 1, step, 0)

    nb = pn // (2 * yn)
    depth = w.shape[0]
    cosine = cosbuf[...].reshape(2 * t_rows, HEAD)
    sine = sinbuf[...].reshape(2 * t_rows, HEAD)

    def project(part):
        acc = None
        for n in range(2 * yn):
            left = tokbuf[n].reshape(2 * t_rows, tok.shape[1])
            right = wbuf[part, n * nb : (n + 1) * nb].reshape(nb * depth, HEAD)
            term = jnp.dot(left, right, preferred_element_type=F32)
            acc = term if acc is None else acc + term
        return acc

    def rotate(v):
        return v * cosine + pltpu.roll(v, HEAD // 2, 1) * sine

    codes = jnp.concatenate([metabuf[0, i, 0:1, :] + 4 * i for i in range(2)], axis=1)
    slots = iota((8 * pn, 2 * t_rows), 0)
    onehot = (slots == codes).astype(F32).astype(BF)
    for h in range(2):
        if h and last:
            for part in range(1, PARTS):
                ring(last, part)
        took(wbuf.at[h, pl.ds(0, 2 * zn)], pr.at[h])
        q = rotate(project(h)).astype(BF)
        packed = jnp.dot(onehot, q, preferred_element_type=F32)
        qsend[h] = packed.reshape(pn, 8, HEAD).astype(BF)

        def send_query(p, h=h):
            remote(
                qsend.at[h, p],
                qrecv.at[h, z * 2 + c, jx],
                qs.at[h],
                qr.at[h],
                {"wide": p, "narrow": y * 2 + k},
            ).start()

        each_wide(send_query)

        @pl.when(selfcase)
        def _():
            pltpu.make_async_copy(qsend.at[h, wide], qrecv.at[h, z * 2 + c, jx], qloc.at[h]).start()

        @pl.when(jnp.logical_not(selfcase))
        def _():
            send_query(wide)

        for i in range(2):
            hsend[i, :, h * HEAD : (h + 1) * HEAD] = q[i * t_rows : (i + 1) * t_rows]

    took(wbuf.at[2, pl.ds(0, 2 * zn)], pr.at[2])
    third = project(2)
    third = jnp.where(jx == 0, rotate(third), third).astype(BF)
    for i in range(2):
        hsend[i, :, 2 * HEAD :] = third[i * t_rows : (i + 1) * t_rows]

    def home(i):
        src, dst, rsem = hsend.at[i], hrecv.at[jx], hr.at[jx]
        return (
            lambda: remote(src, dst, hs.at[i], rsem, dev(2 * c + i, z, y, k)),
            lambda: pltpu.make_async_copy(src, dst, rsem),
        )

    for i in range(2):
        either(home(i), selfcase & (jx == i))

    kcopy.wait()
    vcopy.wait()
    took(limsend.at[pl.ds(0, pn - 1)], ais.at[0])
    took(limsend.at[pl.ds(0, pn - 1)], air.at[0])
    own_limit.wait()

    rows_all = 4 * pn
    lim_rows = limrecv[...].reshape(pn, HEAD).astype(BF)
    owner = (iota((rows_all, pn), 0) // 4 == iota((rows_all, pn), 1)).astype(F32).astype(BF)
    lim_all = jnp.dot(owner, lim_rows, preferred_element_type=F32)
    rlane, rsub = iota((rows_all, HEAD), 1), iota((rows_all, HEAD), 0) % 4
    pick = jnp.where(rlane == rsub, 64.0, jnp.where(rlane == rsub + 4, 1.0, 0.0))
    limit = jnp.sum(lim_all * pick, axis=1, keepdims=True).astype(I32)

    scale = 1.0 / HEAD**0.5
    length = kbuf.shape[0]
    allowed = iota((rows_all, length), 1) < limit
    lse_all = jnp.zeros((rows_all, HEAD), F32)
    low8 = iota((2 * zn, 8, HEAD), 1) < 4
    gather4 = (iota((pn, rows_all), 1) // 4 == iota((pn, rows_all), 0)).astype(F32)

    def own_result(h):
        return pltpu.make_async_copy(fsend.at[h, jx, z * 2 + k], frecv.at[h, wide], floc.at[h])

    own_lse = pltpu.make_async_copy(lsend.at[z * XS + x], lrecv.at[wide], loc.at[1])
    for h in range(2):

        @pl.when(selfcase)
        def _():
            pltpu.make_async_copy(qsend.at[h, wide], qrecv.at[h, z * 2 + c, jx], qloc.at[h]).wait()
            took(qsend.at[h, pl.ds(0, pn - 1)], qs.at[h])
            took(qsend.at[h, pl.ds(0, pn - 1)], qr.at[h])

        @pl.when(jnp.logical_not(selfcase))
        def _():
            took(qsend.at[h], qs.at[h])
            took(qsend.at[h], qr.at[h])

        halves_out = []
        for j in range(2):
            q = qrecv[h, :, j].astype(F32).reshape(rows_all, HEAD).astype(BF)
            s = lax.dot_general(
                q, kbuf[...], (((1,), (1,)), ((), ())), preferred_element_type=F32
            )
            s = jnp.where(allowed, s * scale, -1e30)
            top = jnp.max(s, axis=1, keepdims=True)
            e = jnp.exp(s - top)
            total = jnp.sum(e, axis=1, keepdims=True)
            o = jnp.dot(e.astype(BF), vbuf[...], preferred_element_type=F32) / total
            lse = top + jnp.log(total)
            lse_all = jnp.where(rlane == (2 * j + h) * 4 + rsub, lse, lse_all)
            halves_out.append(o.reshape(2 * zn, 8, HEAD))
        a, b = halves_out
        ra, rb = pltpu.roll(a, 4, 1), pltpu.roll(b, 4, 1)
        fsend[h, 0] = jnp.where(low8, a, rb).astype(BF)
        fsend[h, 1] = jnp.where(low8, ra, b).astype(BF)
        if h == 1:
            lses = jnp.dot(gather4, lse_all, preferred_element_type=F32, precision=HI)
            lsend[...] = lses.reshape(pn, 1, HEAD)

        def send_result(p, h=h):
            xx, zz = p // zn, p % zn
            where = {"wide": p, "narrow": nar}
            if h == 1:
                remote(lsend.at[zz * XS + xx], lrecv.at[wide], ais.at[1], air.at[1], where).start()
            remote(
                fsend.at[h, xx % 2, zz * 2 + xx // 2], frecv.at[h, wide], fs.at[h], fr.at[h], where
            ).start()

        each_wide(send_result)
        own_result(h).start()
    own_lse.start()

    for i in range(2):
        took(hrecv.at[i], hr.at[i])
    key = hrecv[0, :, 2 * HEAD :].astype(F32)
    value = hrecv[1, :, 2 * HEAD :].astype(F32)
    key_first = jnp.concatenate([key[:reqs], key[:reqs]], axis=0)
    value_first = jnp.concatenate([value[:reqs], value[:reqs]], axis=0)
    second = iota((t_rows, 1), 0) >= reqs
    same, prev = [], []
    for g in range(4):
        q = hrecv[g // 2, :, (g % 2) * HEAD : (g % 2 + 1) * HEAD].astype(F32)
        same.append(jnp.sum(q * key, axis=1, keepdims=True) * scale)
        early = jnp.sum(q * key_first, axis=1, keepdims=True) * scale
        prev.append(jnp.where(second, early, -1e30))
    code = to_column(meta[0:1, :], t_rows)

    for h in range(2):
        took(frecv.at[h, pl.ds(0, pn - 1)], fs.at[h])
        took(frecv.at[h, pl.ds(0, pn - 1)], fr.at[h])
        own_result(h).wait()
    took(lsend.at[pl.ds(0, pn - 1)], ais.at[1])
    took(lrecv.at[pl.ds(0, pn - 1)], air.at[1])
    own_lse.wait()

    far_rows = [frecv[h].astype(F32).reshape(8 * pn, HEAD).astype(BF) for h in range(2)]
    lse_rows = lrecv[...].reshape(pn, HEAD)
    owner_p = (iota((t_rows, pn), 1) == code // 8).astype(F32)
    lse_mine = jnp.dot(owner_p, lse_rows, preferred_element_type=F32, precision=HI)
    slot_cols = iota((t_rows, 8 * pn), 1)
    lane = iota((t_rows, HEAD), 1)
    for j in range(2):
        pickj = (slot_cols == code + 4 * j).astype(F32).astype(BF)
        for h in range(2):
            far = jnp.dot(pickj, far_rows[h], preferred_element_type=F32)
            g = 2 * j + h
            lse = jnp.sum(
                jnp.where(lane == g * 4 + code % 8, lse_mine, 0.0), axis=1, keepdims=True
            )
            top = jnp.maximum(jnp.maximum(lse, same[g]), prev[g])
            ef, es, ep = jnp.exp(lse - top), jnp.exp(same[g] - top), jnp.exp(prev[g] - top)
            total = ef + es + ep
            num = far * ef + value * es + value_first * ep
            out[:, g * HEAD : (g + 1) * HEAD] = (num / total).astype(BF)

    for j in range(2):
        for part in range(PARTS):
            sent(wx(j, part), selfcase & (jx == j))
    for o in range(XS):
        if o:
            routes_to(o)[0]().wait_send()
        else:
            sent(routes_to(o), selfcase)
    for o in yorder:
        if o:
            token(o)[0]().wait_send()
        else:
            sent(token(o), selfcase)

    @pl.when(selfcase)
    def _():
        took(tokbuf, xs)

    took(tokbuf.at[pl.ds(0, yn), 0], xs2)
    if zn > 1:
        took(wbuf.at[:, pl.ds(0, 2 * (zn - 1))], zs)
    took(wbuf.at[:, pl.ds(0, 2 * zn)], ps)
    for i in range(2):
        sent(home(i), selfcase & (jx == i))


def on_device(dims, tokens, qkv_weight, rotated_prefix_keys, shared_prefix_values, prefix_of, positions):
    zn, yn = dims
    pn = XS * zn
    reqs, _, feat = tokens.shape
    t_rows = reqs * STEPS
    depth = qkv_weight.shape[0]
    length = rotated_prefix_keys.shape[1]
    vm = pl.BlockSpec(memory_space=pltpu.VMEM)
    hbm = pl.BlockSpec(memory_space=pl.ANY)
    dma = pltpu.SemaphoreType.DMA
    zmax = max(1, zn // 2)
    V = pltpu.VMEM
    result = pl.pallas_call(
        functools.partial(kernel, dims),
        out_shape=jax.ShapeDtypeStruct((t_rows, 4 * HEAD), BF),
        in_specs=[hbm, hbm, hbm, hbm, vm, vm],
        out_specs=vm,
        scratch_shapes=[
            V((depth, 6 * HEAD), BF),
            V((reqs, STEPS, feat), BF),
            V((t_rows, feat), BF),
            V((PARTS, pn, depth, HEAD), BF),
            V((2 * yn, 2, t_rows, feat), BF),
            V((length, HEAD), BF),
            V((length, HEAD), BF),
            V((8, t_rows), I32),
            V((2, 2, 8, t_rows), I32),
            V((2, t_rows, HEAD), F32),
            V((2, t_rows, HEAD), F32),
            V((pn, 1, HEAD), F32),
            V((pn, 1, HEAD), F32),
            V((2, t_rows, 3 * HEAD), BF),
            V((2, t_rows, 3 * HEAD), BF),
            V((2, pn, 8, HEAD), BF),
            V((2, 2 * zn, 2, 8, HEAD), BF),
            V((2, 2, 2 * zn, 8, HEAD), BF),
            V((2, pn, 8, HEAD), BF),
            V((pn, 1, HEAD), F32),
            V((pn, 1, HEAD), F32),
            dma((2, PARTS)),
            dma((2, PARTS)),
            dma(()),
            dma((2, 2, PARTS, zmax)),
            dma(()),
            dma((PARTS,)),
            dma((yn,)),
            dma((2 * yn,)),
            dma((XS,)),
            dma((2, 2)),
            dma(()),
            dma((2 * yn,)),
            dma(()),
            dma((2 * yn,)),
            *[dma((2,)) for _ in range(11)],
            dma((4,)),
        ],
        compiler_params=pltpu.CompilerParams(
            collective_id=0, has_side_effects=True, vmem_limit_bytes=60 * 2**20
        ),
        name="decode_step",
    )(
        tokens,
        qkv_weight,
        rotated_prefix_keys,
        shared_prefix_values,
        prefix_of.reshape(1, reqs),
        positions.reshape(1, reqs),
    )
    return result.reshape(STEPS, reqs, 4 * HEAD).transpose(1, 0, 2)


def solution(mesh):
    dims = (mesh.shape["wide"] // XS, mesh.shape["narrow"] // 2)
    return jax.shard_map(
        functools.partial(on_device, dims),
        mesh=mesh,
        in_specs=(
            P("wide", None, "narrow"),
            P("wide", "narrow"),
            P("wide", None, "narrow"),
            P("wide", None, "narrow"),
            P("wide", None),
            P("wide"),
        ),
        out_specs=P("wide", None, "narrow"),
        check_vma=False,
    )
```

```python
import functools
import math

import jax
import jax.numpy as jnp
from jax import lax
from jax.experimental import pallas as pl
from jax.experimental.pallas import tpu as pltpu
from jax.sharding import PartitionSpec as P

HEAD = 128
STEPS = 2
XS = 4
PARTS = 3
XAT = 3
MESH = pl.DeviceIdType.MESH
BF = jnp.bfloat16
F32 = jnp.float32
I32 = jnp.int32
HI = lax.Precision.HIGHEST


def iota(shape, dim):
    return lax.broadcasted_iota(I32, shape, dim)


def to_column(row, n):
    eye = iota((n, row.shape[1]), 0) == iota((n, row.shape[1]), 1)
    return jnp.sum(jnp.where(eye, row, 0), axis=1, keepdims=True)


def frequencies():
    lane = iota((1, HEAD), 1) % (HEAD // 2)
    high, low = lane // 8, lane % 8
    a = jnp.full((1, HEAD), 1.0, F32)
    b = jnp.full((1, HEAD), 1.0, F32)
    for t in range(1, 8):
        a = jnp.where(high == t, 10000.0 ** (-8 * t / 64), a)
        b = jnp.where(low == t, 10000.0 ** (-t / 64), b)
    return a * b


def kernel(
    dims,
    traw,
    w,
    keys,
    vals,
    pref,
    pos,
    out,
    tokin,
    tok,
    wbuf,
    tokbuf,
    kbuf,
    vbuf,
    meta,
    metabuf,
    cosbuf,
    sinbuf,
    limsend,
    limrecv,
    hsend,
    hrecv,
    qsend,
    qrecv,
    fsend,
    frecv,
    lsend,
    lrecv,
    farbuf,
    wxs,
    wxr,
    zs,
    zr,
    ps,
    pr,
    t1s,
    t1r,
    m1s,
    m1r,
    xs,
    xr,
    xs2,
    xr2,
    kvs,
    hs,
    hr,
    qs,
    qr,
    qloc,
    fs,
    fr,
    floc,
    ais,
    air,
    loc,
):
    zn, yn = dims
    pn = XS * zn
    t_rows = tok.shape[0]
    reqs = t_rows // STEPS
    wide, nar = lax.axis_index("wide"), lax.axis_index("narrow")
    x, z = wide // zn, wide % zn
    y, c = nar // 2, nar % 2
    k, jx = x // 2, x % 2
    selfcase = k == c

    def dev(xx, zz, yy, cc):
        return {"wide": xx * zn + zz, "narrow": yy * 2 + cc}

    def remote(src, dst, ss, rs, where):
        return pltpu.make_async_remote_copy(
            src_ref=src, dst_ref=dst, send_sem=ss, recv_sem=rs, device_id=where, device_id_type=MESH
        )

    def took(ref, sem):
        pltpu.make_async_copy(ref, ref, sem).wait()

    up_z, down_z = (z + 1) % zn, (z + zn - 1) % zn

    barrier = pltpu.get_barrier_semaphore()
    peers = [dev((x + o) % XS, z, y, (c + d) % 2) for o in range(XS) for d in range(2) if o or d]
    if zn > 1:
        peers += [dev(x, up_z, y, c), dev(x, down_z, y, c)]
    if yn > 1:
        peers += [dev(x, z, (y + o) % yn, (c + d) % 2) for o in range(1, yn) for d in range(2)]
    for peer in peers:
        pl.semaphore_signal(barrier, inc=1, device_id=peer, device_id_type=MESH)

    kcopy = pltpu.make_async_copy(keys.at[0], kbuf, kvs.at[0])
    vcopy = pltpu.make_async_copy(vals.at[0], vbuf, kvs.at[1])
    kcopy.start()
    vcopy.start()

    tcopy = pltpu.make_async_copy(traw, tokin, loc.at[3])
    tcopy.start()
    pl.semaphore_wait(barrier, len(peers))

    def wx(j, part):
        start = 4 * HEAD + HEAD * j if part == 2 else HEAD * (2 * j + part)
        src = w.at[:, pl.ds(start, HEAD)]
        dst = wbuf.at[part, wide]
        rsem = wxr.at[jx, part]
        return (
            lambda: remote(src, dst, wxs.at[j, part], rsem, dev(2 * c + j, z, y, k)),
            lambda: pltpu.make_async_copy(src, dst, rsem),
        )

    def either(pair, is_self):
        @pl.when(is_self)
        def _():
            pair[1]().start()

        @pl.when(jnp.logical_not(is_self))
        def _():
            pair[0]().start()

    def sent(pair, is_self):
        @pl.when(jnp.logical_not(is_self))
        def _():
            pair[0]().wait_send()

    for part in range(PARTS):
        for j in range(2):
            either(wx(j, part), selfcase & (jx == j))

    tcopy.wait()
    for step in range(STEPS):
        tok[step * reqs : (step + 1) * reqs] = tokin[:, step, :]

    def token(o):
        dst, rsem = tokbuf.at[nar, jx], t1r.at[nar]
        return (
            lambda: remote(tok, dst, t1s.at[o], rsem, dev(x, z, (y + o) % yn, k)),
            lambda: pltpu.make_async_copy(tok, dst, rsem),
        )

    yorder = [0, 1, 3, 2] if yn == 4 else list(range(yn))
    for o in yorder:
        if o:
            token(o)[0]().start()
        else:
            either(token(o), selfcase)

    pcol = to_column(pref[...], reqs)
    before = (pcol == pref[...]) & (iota((reqs, reqs), 0) < iota((reqs, reqs), 1))
    rank = jnp.sum(before.astype(I32), axis=0, keepdims=True)
    code_col = to_column(pref[...] * 8 + rank * 2, reqs)
    pos_col = to_column(pos[...], reqs)
    spread = iota((reqs, t_rows), 0) == iota((reqs, t_rows), 1) % reqs
    step_lane = iota((1, t_rows), 1) // reqs
    code_row = jnp.sum(jnp.where(spread, code_col, 0), axis=0, keepdims=True) + step_lane
    place_row = jnp.sum(jnp.where(spread, pos_col, 0), axis=0, keepdims=True) + step_lane
    which = iota((8, t_rows), 0)
    meta[...] = jnp.where(which == 0, code_row, jnp.where(which == 1, place_row, 0))


    def routes_to(o):
        dst, rsem = metabuf.at[c, jx], m1r.at[c, jx]
        return (
            lambda: remote(meta, dst, m1s.at[o], rsem, dev((x + o) % XS, z, y, k)),
            lambda: pltpu.make_async_copy(meta, dst, rsem),
        )

    for o in range(XS):
        if o:
            routes_to(o)[0]().start()
        else:
            either(routes_to(o), selfcase)

    lane = iota((reqs, HEAD), 1)
    halves = jnp.where(lane < 4, pos_col // 64, pos_col % 64).astype(F32).astype(BF)
    code64 = pref[...] * 8 + rank * 2
    prow = iota((pn, reqs), 0) * 8
    lim = [
        jnp.dot(
            (code64 == prow + 2 * u).astype(F32).astype(BF), halves, preferred_element_type=F32
        )
        for u in range(2)
    ]
    limits = jnp.where((iota((pn, HEAD), 1) // 2) % 2 == 0, lim[0], lim[1])
    limsend[...] = limits.reshape(pn, 1, HEAD)

    def send_limit(xx, zz):
        remote(
            limsend.at[xx * zn + zz],
            limrecv.at[z * XS + x],
            ais.at[0],
            air.at[0],
            dev(xx, zz, y, c),
        ).start()

    own_limit = pltpu.make_async_copy(limsend.at[wide], limrecv.at[z * XS + x], loc.at[0])
    own_limit.start()
    for o in range(1, XS):
        send_limit((x + o) % XS, z)

    near = jnp.where(selfcase, jx, 1 - jx)
    block = (near, 1 - near)

    def reach(n):
        return {(0, 0): n // 2, (0, 1): (n - 1) // 2, (1, 0): (n - 1) // 2, (1, 1): n // 2}

    zreach, last = reach(zn), zn // 2
    zto = (up_z, down_z)

    def zslot(direction, a, d):
        origin = (z + zn - d) % zn if direction == 0 else (z + d) % zn
        return (2 * c + block[a]) * zn + origin

    def zsend(direction, a, part, d):
        ref = wbuf.at[part, zslot(direction, a, d)]
        remote(ref, ref, zs, zr.at[direction, a, part, d], dev(x, zto[direction], y, c)).start()
        if d + 1 == last > 1:
            remote(ref, ref, ps, pr.at[part], dev(x, zto[direction], y, 1 - c)).start()

    def partner(direction, a, part, d):
        ref = wbuf.at[part, zslot(direction, a, d)]
        remote(ref, ref, ps, pr.at[part], dev(x, z, y, 1 - c)).start()

    order = [((y + o) % yn) * 2 + (c + cc) % 2 for o in yorder for cc in range(2)]
    plus = selfcase == (jx == 1)
    ahead = jnp.where(plus, (x + 1) % XS, (x + XS - 1) % XS)
    behind = jnp.where(plus, (x + XS - 1) % XS, (x + 1) % XS)
    onward = jnp.where(plus, 0, 1)

    def own_rows(m):
        @pl.when(selfcase)
        def _():
            ref = tokbuf.at[order[m], jx]
            took(ref, t1r.at[order[m]])
            for side in (1, XS - 1):
                remote(ref, ref, xs, xr.at[order[m]], dev((x + side) % XS, z, y, c)).start()

    def next_rows(m):
        ref = tokbuf.at[order[m], behind % 2]
        took(ref, xr.at[order[m]])

        @pl.when(order[m] % 2 == onward)
        def _():
            remote(ref, ref, xs2, xr2.at[order[m]], dev(ahead, z, y, c)).start()

    for a in range(2):
        for part in range(PARTS):
            took(wbuf.at[part, zslot(0, a, 0)], wxr.at[block[a], part])
            for direction in range(2):
                if zreach[direction, a] > 0:
                    zsend(direction, a, part, 0)
            partner(0, a, part, 0)
        for m in range(2):
            if 2 * a + m < 2 * yn:
                own_rows(2 * a + m)

    def angles():
        freq = frequencies()
        for i in range(2):
            for cc in range(2):
                took(metabuf.at[cc, i], m1r.at[cc, i])
            place = to_column(metabuf[0, i, 1:2, :], t_rows).astype(F32)
            angle = place * freq
            low = iota((t_rows, HEAD), 1) < HEAD // 2
            sine = jnp.sin(angle)
            cosbuf[i] = jnp.cos(angle)
            sinbuf[i] = jnp.where(low, -sine, sine)

    rest = list(range(4, 2 * yn))
    coming = list(range(2 * yn))

    def ring(d, part):
        for a in range(2):
            for direction in range(2):
                if d <= zreach[direction, a]:
                    took(
                        wbuf.at[part, zslot(direction, a, d)],
                        zr.at[direction, a, part, d - 1],
                    )
                    if d < zreach[direction, a]:
                        zsend(direction, a, part, d)
                    if d < last or last == 1:
                        partner(direction, a, part, d)

    for d in range(1, last + 1):
        for part in range(PARTS):
            if d < last or part == 0:
                ring(d, part)
        for o in range(XS):
            send_limit((x + o) % XS, (z + zn - d) % zn)
            if d <= (zn - 1) // 2:
                send_limit((x + o) % XS, (z + d) % zn)
        for m in rest[:2]:
            own_rows(m)
        rest = rest[2:]
        if d == 1:
            angles()
        if d >= XAT:
            for m in coming[:2]:
                next_rows(m)
            coming = coming[2:]
    for m in rest:
        own_rows(m)
    for m in coming:
        next_rows(m)

    @pl.when(jnp.logical_not(selfcase))
    def _():
        for m in range(2 * yn):
            took(tokbuf.at[order[m], 1 - behind % 2], xr2.at[order[m]])

    def each_wide(fn):
        half = zn // 2

        def step(t, carry):
            lap = t // XS
            away = half - (lap + 1) // 2
            dz = jnp.where(lap % 2 == 1, away, (zn - away) % zn)
            fn(((x + t + 1) % XS) * zn + (z + dz) % zn)
            return carry

        lax.fori_loop(0, pn - 1, step, 0)

    nb = pn // (2 * yn)
    depth = w.shape[0]
    cosine = cosbuf[...].reshape(2 * t_rows, HEAD)
    sine = sinbuf[...].reshape(2 * t_rows, HEAD)

    def project(part):
        acc = None
        for n in range(2 * yn):
            left = tokbuf[n].reshape(2 * t_rows, tok.shape[1])
            right = wbuf[part, n * nb : (n + 1) * nb].reshape(nb * depth, HEAD)
            term = jnp.dot(left, right, preferred_element_type=F32)
            acc = term if acc is None else acc + term
        return acc

    def rotate(v):
        return v * cosine + pltpu.roll(v, HEAD // 2, 1) * sine

    codes = jnp.concatenate([metabuf[0, i, 0:1, :] + 4 * i for i in range(2)], axis=1)
    slots = iota((8 * pn, 2 * t_rows), 0)
    onehot = (slots == codes).astype(F32).astype(BF)
    for h in range(2):
        if h and last:
            for part in range(1, PARTS):
                ring(last, part)
        took(wbuf.at[h, pl.ds(0, 2 * zn)], pr.at[h])
        q = rotate(project(h)).astype(BF)
        packed = jnp.dot(onehot, q, preferred_element_type=F32)
        qsend[h] = packed.reshape(pn, 8, HEAD).astype(BF)

        def send_query(p, h=h):
            remote(
                qsend.at[h, p],
                qrecv.at[h, z * 2 + c, jx],
                qs.at[h],
                qr.at[h],
                {"wide": p, "narrow": y * 2 + k},
            ).start()

        each_wide(send_query)

        @pl.when(selfcase)
        def _():
            pltpu.make_async_copy(qsend.at[h, wide], qrecv.at[h, z * 2 + c, jx], qloc.at[h]).start()

        @pl.when(jnp.logical_not(selfcase))
        def _():
            send_query(wide)

        for i in range(2):
            hsend[i, :, h * HEAD : (h + 1) * HEAD] = q[i * t_rows : (i + 1) * t_rows]

    took(wbuf.at[2, pl.ds(0, 2 * zn)], pr.at[2])
    third = project(2)
    third = jnp.where(jx == 0, rotate(third), third).astype(BF)
    for i in range(2):
        hsend[i, :, 2 * HEAD :] = third[i * t_rows : (i + 1) * t_rows]

    def home(i):
        src, dst, rsem = hsend.at[i], hrecv.at[jx], hr.at[jx]
        return (
            lambda: remote(src, dst, hs.at[i], rsem, dev(2 * c + i, z, y, k)),
            lambda: pltpu.make_async_copy(src, dst, rsem),
        )

    for i in range(2):
        either(home(i), selfcase & (jx == i))

    kcopy.wait()
    vcopy.wait()
    took(limsend.at[pl.ds(0, pn - 1)], ais.at[0])
    took(limsend.at[pl.ds(0, pn - 1)], air.at[0])
    own_limit.wait()

    rows_all = 4 * pn
    lim_rows = limrecv[...].reshape(pn, HEAD).astype(BF)
    owner = (iota((rows_all, pn), 0) // 4 == iota((rows_all, pn), 1)).astype(F32).astype(BF)
    lim_all = jnp.dot(owner, lim_rows, preferred_element_type=F32)
    rlane, rsub = iota((rows_all, HEAD), 1), iota((rows_all, HEAD), 0) % 4
    pick = jnp.where(rlane == rsub, 64.0, jnp.where(rlane == rsub + 4, 1.0, 0.0))
    limit = jnp.sum(lim_all * pick, axis=1, keepdims=True).astype(I32)

    scale = 1.0 / HEAD**0.5
    length = kbuf.shape[0]
    allowed = iota((rows_all, length), 1) < limit
    lse_all = jnp.zeros((rows_all, HEAD), F32)
    low8 = iota((2 * zn, 8, HEAD), 1) < 4
    gather4 = (iota((pn, rows_all), 1) // 4 == iota((pn, rows_all), 0)).astype(F32)

    def own_result(h):
        return pltpu.make_async_copy(fsend.at[h, jx, z * 2 + k], frecv.at[h, wide], floc.at[h])

    own_lse = pltpu.make_async_copy(lsend.at[z * XS + x], lrecv.at[wide], loc.at[1])
    for h in range(2):

        @pl.when(selfcase)
        def _():
            pltpu.make_async_copy(qsend.at[h, wide], qrecv.at[h, z * 2 + c, jx], qloc.at[h]).wait()
            took(qsend.at[h, pl.ds(0, pn - 1)], qs.at[h])
            took(qsend.at[h, pl.ds(0, pn - 1)], qr.at[h])

        @pl.when(jnp.logical_not(selfcase))
        def _():
            took(qsend.at[h], qs.at[h])
            took(qsend.at[h], qr.at[h])

        halves_out = []
        for j in range(2):
            q = qrecv[h, :, j].astype(F32).reshape(rows_all, HEAD).astype(BF)
            s = lax.dot_general(
                q, kbuf[...], (((1,), (1,)), ((), ())), preferred_element_type=F32
            )
            s = jnp.where(allowed, s * scale, -1e30)
            top = jnp.max(s, axis=1, keepdims=True)
            e = jnp.exp(s - top)
            total = jnp.sum(e, axis=1, keepdims=True)
            o = jnp.dot(e.astype(BF), vbuf[...], preferred_element_type=F32) / total
            lse = top + jnp.log(total)
            lse_all = jnp.where(rlane == (2 * j + h) * 4 + rsub, lse, lse_all)
            halves_out.append(o.reshape(2 * zn, 8, HEAD))
        a, b = halves_out
        ra, rb = pltpu.roll(a, 4, 1), pltpu.roll(b, 4, 1)
        fsend[h, 0] = jnp.where(low8, a, rb).astype(BF)
        fsend[h, 1] = jnp.where(low8, ra, b).astype(BF)
        if h == 1:
            lses = jnp.dot(gather4, lse_all, preferred_element_type=F32, precision=HI)
            lsend[...] = lses.reshape(pn, 1, HEAD)

        def send_result(p, h=h):
            xx, zz = p // zn, p % zn
            where = {"wide": p, "narrow": nar}
            if h == 1:
                remote(lsend.at[zz * XS + xx], lrecv.at[wide], ais.at[1], air.at[1], where).start()
            remote(
                fsend.at[h, xx % 2, zz * 2 + xx // 2], frecv.at[h, wide], fs.at[h], fr.at[h], where
            ).start()

        each_wide(send_result)
        own_result(h).start()
    own_lse.start()

    for i in range(2):
        took(hrecv.at[i], hr.at[i])
    key = hrecv[0, :, 2 * HEAD :].astype(F32)
    value = hrecv[1, :, 2 * HEAD :].astype(F32)
    key_first = jnp.concatenate([key[:reqs], key[:reqs]], axis=0)
    value_first = jnp.concatenate([value[:reqs], value[:reqs]], axis=0)
    second = iota((t_rows, 1), 0) >= reqs
    same, prev = [], []
    for g in range(4):
        q = hrecv[g // 2, :, (g % 2) * HEAD : (g % 2 + 1) * HEAD].astype(F32)
        same.append(jnp.sum(q * key, axis=1, keepdims=True) * scale)
        early = jnp.sum(q * key_first, axis=1, keepdims=True) * scale
        prev.append(jnp.where(second, early, -1e30))
    code = to_column(meta[0:1, :], t_rows)

    owner_p = (iota((t_rows, pn), 1) == code // 8).astype(F32)
    slot_cols = iota((t_rows, 8 * pn), 1)
    lane = iota((t_rows, HEAD), 1)
    picks = [(slot_cols == code + 4 * j).astype(F32).astype(BF) for j in range(2)]
    for h in range(2):
        took(frecv.at[h, pl.ds(0, pn - 1)], fs.at[h])
        took(frecv.at[h, pl.ds(0, pn - 1)], fr.at[h])
        own_result(h).wait()
        far_rows = frecv[h].astype(F32).reshape(8 * pn, HEAD).astype(BF)
        for j in range(2):
            farbuf[2 * j + h] = jnp.dot(picks[j], far_rows, preferred_element_type=F32)
    took(lsend.at[pl.ds(0, pn - 1)], ais.at[1])
    took(lrecv.at[pl.ds(0, pn - 1)], air.at[1])
    own_lse.wait()

    lse_rows = lrecv[...].reshape(pn, HEAD)
    lse_mine = jnp.dot(owner_p, lse_rows, preferred_element_type=F32, precision=HI)
    for g in range(4):
        lse = jnp.sum(jnp.where(lane == g * 4 + code % 8, lse_mine, 0.0), axis=1, keepdims=True)
        top = jnp.maximum(jnp.maximum(lse, same[g]), prev[g])
        ef, es, ep = jnp.exp(lse - top), jnp.exp(same[g] - top), jnp.exp(prev[g] - top)
        total = ef + es + ep
        num = farbuf[g] * ef + value * es + value_first * ep
        out[:, g * HEAD : (g + 1) * HEAD] = (num / total).astype(BF)

    for j in range(2):
        for part in range(PARTS):
            sent(wx(j, part), selfcase & (jx == j))
    for o in range(XS):
        if o:
            routes_to(o)[0]().wait_send()
        else:
            sent(routes_to(o), selfcase)
    for o in yorder:
        if o:
            token(o)[0]().wait_send()
        else:
            sent(token(o), selfcase)

    @pl.when(selfcase)
    def _():
        took(tokbuf, xs)

    took(tokbuf.at[pl.ds(0, yn), 0], xs2)
    if zn > 1:
        took(wbuf.at[:, pl.ds(0, 2 * (zn - 1))], zs)
    took(wbuf.at[:, pl.ds(0, 2 * zn)], ps)
    for i in range(2):
        sent(home(i), selfcase & (jx == i))


def on_device(dims, tokens, qkv_weight, rotated_prefix_keys, shared_prefix_values, prefix_of, positions):
    zn, yn = dims
    pn = XS * zn
    reqs, _, feat = tokens.shape
    t_rows = reqs * STEPS
    depth = qkv_weight.shape[0]
    length = rotated_prefix_keys.shape[1]
    vm = pl.BlockSpec(memory_space=pltpu.VMEM)
    hbm = pl.BlockSpec(memory_space=pl.ANY)
    dma = pltpu.SemaphoreType.DMA
    zmax = max(1, zn // 2)
    V = pltpu.VMEM
    result = pl.pallas_call(
        functools.partial(kernel, dims),
        out_shape=V((t_rows, 4 * HEAD), BF),
        in_specs=[hbm, hbm, hbm, hbm, vm, vm],
        out_specs=vm,
        scratch_shapes=[
            V((reqs, STEPS, feat), BF),
            V((t_rows, feat), BF),
            V((PARTS, pn, depth, HEAD), BF),
            V((2 * yn, 2, t_rows, feat), BF),
            V((length, HEAD), BF),
            V((length, HEAD), BF),
            V((8, t_rows), I32),
            V((2, 2, 8, t_rows), I32),
            V((2, t_rows, HEAD), F32),
            V((2, t_rows, HEAD), F32),
            V((pn, 1, HEAD), F32),
            V((pn, 1, HEAD), F32),
            V((2, t_rows, 3 * HEAD), BF),
            V((2, t_rows, 3 * HEAD), BF),
            V((2, pn, 8, HEAD), BF),
            V((2, 2 * zn, 2, 8, HEAD), BF),
            V((2, 2, 2 * zn, 8, HEAD), BF),
            V((2, pn, 8, HEAD), BF),
            V((pn, 1, HEAD), F32),
            V((pn, 1, HEAD), F32),
            V((4, t_rows, HEAD), F32),
            dma((2, PARTS)),
            dma((2, PARTS)),
            dma(()),
            dma((2, 2, PARTS, zmax)),
            dma(()),
            dma((PARTS,)),
            dma((yn,)),
            dma((2 * yn,)),
            dma((XS,)),
            dma((2, 2)),
            dma(()),
            dma((2 * yn,)),
            dma(()),
            dma((2 * yn,)),
            *[dma((2,)) for _ in range(11)],
            dma((4,)),
        ],
        compiler_params=pltpu.CompilerParams(
            collective_id=0, has_side_effects=True, vmem_limit_bytes=60 * 2**20
        ),
        name="decode_step",
    )(
        tokens,
        qkv_weight,
        rotated_prefix_keys,
        shared_prefix_values,
        prefix_of.reshape(1, reqs),
        positions.reshape(1, reqs),
    )
    return result.reshape(STEPS, reqs, 4 * HEAD).transpose(1, 0, 2)


def solution(mesh):
    dims = (mesh.shape["wide"] // XS, mesh.shape["narrow"] // 2)
    return jax.shard_map(
        functools.partial(on_device, dims),
        mesh=mesh,
        in_specs=(
            P("wide", None, "narrow"),
            P("wide", "narrow"),
            P("wide", None, "narrow"),
            P("wide", None, "narrow"),
            P("wide", None),
            P("wide"),
        ),
        out_specs=P("wide", None, "narrow"),
        check_vma=False,
    )
```
